256 devices in a mesh: cluster: 16 (over z_lo, x), narrow: 16 (over y, z_hi, core).
Axes of the slice: x: 4, y: 4, z: 8 (z_hi: 2, z_lo: 4; z = z_hi * 4 + z_lo), core: 2. Of those that a mesh axis runs over, the one named last changes fastest.
Arguments:
- edge_feats: bfloat16 [524288, 512], P(('cluster', 'narrow')), may hold values from -6 to 6
- cotangent: bfloat16 [524288, 512], P(('cluster', 'narrow')), may hold values from -6 to 6
- down_weight: bfloat16 [512, 64], replicated, may hold values from -0.25 to 0.25
- up_weight: bfloat16 [64, 512], replicated, may hold values from -0.75 to 0.75
- inner_weight: bfloat16 [1, 512, 512], replicated, may hold values from -0.25 to 0.25
- outer_weight: bfloat16 [1, 512, 512], replicated, may hold values from -0.25 to 0.25
- angular: bfloat16 [8192, 8, 4096], P(('cluster', 'narrow')), may hold values from -0.375 to 0.375
- reverse: int32 [524288], P(('cluster', 'narrow')), may hold values from 0 to 524287, as said below
- sources: int32 [8192, 8], P(('cluster', 'narrow')), may hold values from 0 to 8191, as said below
- counts: int32 [8192], P(('cluster', 'narrow')), may hold values from 1 to 8
Outputs:
- output: bfloat16 [524288, 512], P(('cluster', 'narrow'))
- grad_x: bfloat16 [524288, 512], P(('cluster', 'narrow'))
The draws below stay inside these ranges and needn't reach their ends.
Inputs may be any that keep to these rules, and one draw needn't show every extreme that they name: reverse is an involution without fixed points, and reverse[e] // 2048 == ((e + 262144) % 524288) // 2048. sources[k, s] // 512 == k // 512; among the slots of the blocks of one device (blocks m * 32 to (m + 1) * 32 - 1), exactly 16 name a block j with (j % 512) // 32 == i, for every i below 16; slots s >= counts[k] hold valid block numbers that are not used.
All inputs are finite; a program needn't handle non-finite values.
Results may differ from the reference program's by a relative error of at most 0.0075.
Values may be sent and summed in bfloat16 or wider, within the bound.
A program may use at most 128 MiB of HBM per device.

```python
import jax
import jax.numpy as jnp
from jax import lax

D = 512
TRIP = 64
BLK = 64
SEL = 8
RES = 1
E_DEV = 2048
EDGES = 524288
BLOCKS = 8192
CL_BLOCKS = 512
HALF = 262144
PAIRS = 128


def draw_reverse(key, part):
    pair_keys = jax.random.split(key, PAIRS)
    shuffles = jax.vmap(lambda subkey: jax.random.permutation(subkey, E_DEV))(pair_keys).astype(jnp.int32)
    inverse = jnp.argsort(shuffles, axis=1).astype(jnp.int32)
    pair_base = jnp.arange(PAIRS, dtype=jnp.int32)[:, None] * E_DEV
    lower_half = pair_base + shuffles + HALF
    upper_half = pair_base + inverse
    return jnp.concatenate([lower_half.reshape(-1), upper_half.reshape(-1)]).astype(jnp.int32)


def draw_sources(key, part):
    per_device = E_DEV // BLK
    device_count = BLOCKS // per_device
    slot_total = per_device * SEL
    lane_total = CL_BLOCKS // per_device
    perm_keys = jax.random.split(jax.random.fold_in(key, 3), device_count)
    shuffles = jax.vmap(lambda subkey: jax.random.permutation(subkey, slot_total))(perm_keys).astype(jnp.int32)
    lanes = shuffles % lane_total
    within = jax.random.randint(jax.random.fold_in(key, 5), (device_count, slot_total), 0, per_device).astype(jnp.int32)
    device_ids = jnp.arange(device_count, dtype=jnp.int32)[:, None]
    base_block = device_ids * per_device // CL_BLOCKS * CL_BLOCKS
    chosen = base_block + lanes * per_device + within
    return chosen.reshape(BLOCKS, SEL).astype(jnp.int32)


def draw_counts(key, part):
    per_device = E_DEV // BLK
    level_key = jax.random.fold_in(key, 7)
    count_key = jax.random.fold_in(key, 11)
    levels = jax.random.randint(level_key, (BLOCKS // per_device, 1), 1, SEL + 1).astype(jnp.int32)
    levels = jnp.broadcast_to(levels, (BLOCKS // per_device, per_device)).reshape(BLOCKS)
    drawn = jax.random.randint(count_key, (BLOCKS,), 1, levels + 1).astype(jnp.int32)
    drawn = drawn.at[0].set(SEL)
    drawn = drawn.at[1].set(1)
    return drawn.astype(jnp.int32)


def block_scale(stream_key, shape, cuts, smallest, largest):
    def one(axis_at, parts):
        draws = jax.random.uniform(jax.random.fold_in(jax.random.fold_in(stream_key, 6), axis_at), (parts,), jnp.float32, smallest / len(cuts), largest / len(cuts))
        return jnp.repeat(jnp.exp(draws), shape[axis_at] // parts).reshape((-1,) + (1,) * (len(shape) - axis_at - 1))

    gain = one(*cuts[0])
    for cut in cuts[1:]:
        gain = gain * one(*cut)
    return gain


def normal_values(rng, extent, width, limit, shards=(), kind=jnp.bfloat16):
    array = jax.random.normal(rng, extent, jnp.float32) * width
    if len(shards) > 0:
        array = block_scale(rng, extent, shards, -0.22, 0.18) * array
    return jnp.clip(array, min=-limit, max=limit).astype(kind)


def setup_inputs(seed: int = 0) -> dict:
    arg_keys = jax.random.split(jax.random.key(seed), 11)
    return {
        "edge_feats": normal_values(arg_keys[0], (EDGES, D), 1.0, 6.0, ((0, 256),)),
        "cotangent": normal_values(arg_keys[1], (EDGES, D), 1.0, 6.0, ((0, 256),)),
        "down_weight": normal_values(arg_keys[2], (D, TRIP), D ** -0.5, 0.25),
        "up_weight": normal_values(arg_keys[3], (TRIP, D), TRIP ** -0.5, 0.75),
        "inner_weight": normal_values(arg_keys[4], (RES, D, D), D ** -0.5, 0.25),
        "outer_weight": normal_values(arg_keys[5], (RES, D, D), D ** -0.5, 0.25),
        "angular": normal_values(arg_keys[6], (BLOCKS, SEL, BLK * BLK), (BLK * 4) ** -0.5, 0.375, ((0, 256),)),
        "reverse": draw_reverse(jax.random.fold_in(arg_keys[10], 71), 0),
        "sources": draw_sources(jax.random.fold_in(arg_keys[10], 71), 0),
        "counts": draw_counts(jax.random.fold_in(arg_keys[10], 71), 0),
    }


ROOT_HALF = 0.7071067811865476

def silu_grad(pre_act):
    squash = jax.nn.sigmoid(pre_act)
    return squash * (1.0 + pre_act * (1.0 - squash))

def reference(edge_feats, cotangent, down_weight, up_weight, inner_weight, outer_weight, angular, reverse, sources, counts):
    per_group = E_DEV // BLK
    group_count = BLOCKS // per_group
    pre_down = jnp.dot(edge_feats, down_weight, preferred_element_type=jnp.float32)
    trip_feat = jax.nn.silu(pre_down).astype(jnp.bfloat16)
    trip_blocks = trip_feat.reshape(BLOCKS, BLK * TRIP)
    live_mask = (lax.broadcasted_iota(jnp.int32, (BLOCKS, SEL), 1) < counts[:, None]).astype(jnp.float32)
    angle_groups = angular.reshape(group_count, per_group, SEL, BLK, BLK)
    source_groups = sources.reshape(group_count, per_group, SEL)
    mask_groups = live_mask.reshape(group_count, per_group, SEL)

    def forward_group(inputs):
        angle_mats, source_ids, mask_part = inputs
        picked = trip_blocks[source_ids].astype(jnp.float32) * mask_part[:, :, None]
        picked = picked.reshape(per_group, SEL, BLK, TRIP)
        return jnp.einsum('ksij,ksjf->kif', angle_mats.astype(jnp.float32), picked)
    trip_sum = lax.map(forward_group, (angle_groups, source_groups, mask_groups)).reshape(EDGES, TRIP)
    trip_round = trip_sum.astype(jnp.bfloat16)
    pre_up = jnp.dot(trip_round, up_weight, preferred_element_type=jnp.float32)
    up_feat = jax.nn.silu(pre_up).astype(jnp.bfloat16)
    message = (up_feat.astype(jnp.float32) + up_feat[reverse].astype(jnp.float32)) * ROOT_HALF
    hidden_state = (edge_feats.astype(jnp.float32) + message) * ROOT_HALF
    saved_acts = []
    for layer_index in range(RES):
        state_round = hidden_state.astype(jnp.bfloat16)
        pre_in = jnp.dot(state_round, inner_weight[layer_index], preferred_element_type=jnp.float32)
        act_feat = jax.nn.silu(pre_in).astype(jnp.bfloat16)
        pre_out = jnp.dot(act_feat, outer_weight[layer_index], preferred_element_type=jnp.float32)
        saved_acts.append((pre_in, pre_out))
        hidden_state = (hidden_state + jax.nn.silu(pre_out)) * ROOT_HALF
    output = hidden_state.astype(jnp.bfloat16)
    grad_state = cotangent.astype(jnp.float32)
    for layer_index in reversed(range(RES)):
        pre_in, pre_out = saved_acts[layer_index]
        grad_state = grad_state * ROOT_HALF
        grad_out = (grad_state * silu_grad(pre_out)).astype(jnp.bfloat16)
        grad_act = jnp.dot(grad_out, outer_weight[layer_index].T, preferred_element_type=jnp.float32)
        grad_in = (grad_act * silu_grad(pre_in)).astype(jnp.bfloat16)
        grad_state = grad_state + jnp.dot(grad_in, inner_weight[layer_index].T, preferred_element_type=jnp.float32)
    grad_msg = grad_state * ROOT_HALF
    grad_msg_round = grad_msg.astype(jnp.bfloat16)
    grad_up = (grad_msg + grad_msg_round[reverse].astype(jnp.float32)) * ROOT_HALF
    grad_pre_up = (grad_up * silu_grad(pre_up)).astype(jnp.bfloat16)
    grad_trip = jnp.dot(grad_pre_up, up_weight.T, preferred_element_type=jnp.float32).astype(jnp.bfloat16)
    grad_groups = grad_trip.reshape(group_count, per_group, BLK, TRIP)

    def backward_group(accumulated, inputs):
        angle_mats, source_ids, mask_part, grad_part = inputs
        pair_terms = jnp.einsum('ksij,kif->ksjf', angle_mats.astype(jnp.float32), grad_part.astype(jnp.float32))
        pair_terms = pair_terms * mask_part[:, :, None, None]
        accumulated = accumulated.at[source_ids.reshape(-1)].add(pair_terms.reshape(per_group * SEL, BLK * TRIP))
        return (accumulated, None)
    source_grad, ignored = lax.scan(backward_group, jnp.zeros((BLOCKS, BLK * TRIP), jnp.float32), (angle_groups, source_groups, mask_groups, grad_groups))
    source_grad = source_grad.reshape(EDGES, TRIP)
    grad_pre_down = (source_grad * silu_grad(pre_down)).astype(jnp.bfloat16)
    grad_x = grad_msg + jnp.dot(grad_pre_down, down_weight.T, preferred_element_type=jnp.float32)
    return (output, grad_x.astype(jnp.bfloat16))
```

```python
import jax
import jax.numpy as jnp
from jax import lax
from jax.sharding import PartitionSpec as P

ROOT_HALF = 0.7071067811865476


def swapped(array, axis, bit):
    return lax.ppermute(array, axis, [(i, i ^ 1 << bit) for i in range(lax.axis_size(axis))])


def side_by_side(arrays, axis, split_dim, concat_dim, along):
    columns = [a.reshape(*a.shape[:along], -1) for a in arrays]
    both = jnp.concatenate(columns, axis=along)
    result, at, done = (
        lax.all_to_all(both, axis, split_axis=split_dim, concat_axis=concat_dim, tiled=True),
        0,
        [],
    )
    for a, column in zip(arrays, columns):
        slab = result[..., at : at + column.shape[along]]
        done.append(slab.reshape(*slab.shape[:along], *a.shape[along:]))
        at += column.shape[along]
    return tuple(done)


def silu_grad(pre_act):
    squash = jax.nn.sigmoid(pre_act)
    return squash * (1.0 + pre_act * (1.0 - squash))


def dot_trans(operand, matrix):
    return lax.dot_general(
        operand, matrix, (((1,), (1,)), ((), ())), preferred_element_type=jnp.float32
    )


def split_parts(values):
    high_part = values.astype(jnp.bfloat16)
    low_part = (values - high_part.astype(jnp.float32)).astype(jnp.bfloat16)
    return (high_part, low_part)


def on_device(
    edge_feats,
    cotangent,
    down_weight,
    up_weight,
    inner_weight,
    outer_weight,
    angular,
    reverse,
    sources,
    counts,
):
    lane_count = lax.axis_size("narrow")
    top_bit = lax.axis_size("cluster").bit_length() - 2
    local_blocks = counts.shape[0]
    local_edges = edge_feats.shape[0]
    block_edges = local_edges // local_blocks
    trip_width = down_weight.shape[1]
    slot_count = sources.shape[1]
    cluster_blocks = local_blocks * lane_count
    source_local = sources % cluster_blocks
    live_mask = lax.broadcasted_iota(jnp.int32, sources.shape, 1) < counts[:, None]
    rev_slot = reverse % local_edges
    angle_mats = angular.reshape(local_blocks, slot_count, block_edges, block_edges)
    pre_down = jnp.dot(edge_feats, down_weight, preferred_element_type=jnp.float32)
    trip_feat = jax.nn.silu(pre_down).astype(jnp.bfloat16)
    trip_blocks = trip_feat.reshape(local_blocks, block_edges * trip_width)
    shard_piece = lax.all_gather(trip_blocks, "narrow", axis=0, tiled=True)
    columns = lax.broadcasted_iota(jnp.int32, (1, 1, shard_piece.shape[0]), 2)
    selector = ((source_local[:, :, None] == columns) & live_mask[:, :, None]).astype(jnp.bfloat16)
    picked = jnp.einsum("ksp,pf->ksf", selector, shard_piece, preferred_element_type=jnp.float32)
    picked = picked.astype(jnp.bfloat16).reshape(local_blocks, slot_count, block_edges, trip_width)
    trip_sum = jnp.einsum("ksij,ksjf->kif", angle_mats, picked, preferred_element_type=jnp.float32)
    trip_round = trip_sum.reshape(local_edges, trip_width).astype(jnp.bfloat16)
    pre_up = jnp.dot(trip_round, up_weight, preferred_element_type=jnp.float32)
    up_feat = jax.nn.silu(pre_up).astype(jnp.bfloat16)
    partner_trip = swapped(trip_round, "cluster", top_bit)
    partner_pre = jnp.dot(partner_trip[rev_slot], up_weight, preferred_element_type=jnp.float32)
    partner_up = jax.nn.silu(partner_pre).astype(jnp.bfloat16)
    message = (up_feat.astype(jnp.float32) + partner_up.astype(jnp.float32)) * ROOT_HALF
    hidden_state = (edge_feats.astype(jnp.float32) + message) * ROOT_HALF
    layer_index = 0
    state_round = hidden_state.astype(jnp.bfloat16)
    pre_in = jnp.dot(state_round, inner_weight[layer_index], preferred_element_type=jnp.float32)
    act_feat = jax.nn.silu(pre_in).astype(jnp.bfloat16)
    pre_out = jnp.dot(act_feat, outer_weight[layer_index], preferred_element_type=jnp.float32)
    saved_acts = [(pre_in, pre_out)]
    hidden_state = (hidden_state + jax.nn.silu(pre_out)) * ROOT_HALF
    output = hidden_state.astype(jnp.bfloat16)
    grad_state = cotangent.astype(jnp.float32)
    for layer_index in reversed(range(inner_weight.shape[0])):
        pre_in, pre_out = saved_acts[layer_index]
        grad_state = grad_state * ROOT_HALF
        grad_out = (grad_state * silu_grad(pre_out)).astype(jnp.bfloat16)
        grad_act = dot_trans(grad_out, outer_weight[layer_index])
        grad_in = (grad_act * silu_grad(pre_in)).astype(jnp.bfloat16)
        grad_state = grad_state + dot_trans(grad_in, inner_weight[layer_index])
    grad_msg = grad_state * ROOT_HALF
    grad_msg_round = grad_msg.astype(jnp.bfloat16)
    partner_part = (
        grad_msg_round.astype(jnp.float32) * ROOT_HALF * silu_grad(partner_pre)
    ).astype(jnp.bfloat16)
    sent_part = dot_trans(partner_part, up_weight).astype(jnp.bfloat16)
    got_part = swapped(sent_part, "cluster", top_bit)[rev_slot]
    own_part = (grad_msg * ROOT_HALF * silu_grad(pre_up)).astype(jnp.bfloat16)
    grad_trip = (dot_trans(own_part, up_weight) + got_part.astype(jnp.float32)).astype(jnp.bfloat16)
    grad_blocks = grad_trip.reshape(local_blocks, block_edges, trip_width)
    pair_terms = jnp.einsum(
        "ksij,kif->ksjf", angle_mats, grad_blocks, preferred_element_type=jnp.float32
    )
    pair_terms = pair_terms.reshape(local_blocks, slot_count, block_edges * trip_width)
    slot_total = local_blocks * slot_count
    quota = slot_total // lane_count
    flat_terms = (pair_terms * live_mask[:, :, None].astype(jnp.float32)).reshape(
        slot_total, block_edges * trip_width
    )
    owner_lane = (source_local // local_blocks).reshape(slot_total)
    order = jnp.argsort(owner_lane, stable=True)
    sent_terms = flat_terms[order].reshape(lane_count, quota, block_edges * trip_width)
    sent_ids = (
        (source_local % local_blocks)
        .reshape(slot_total)[order]
        .astype(jnp.float32)
        .reshape(lane_count, quota)
    )
    got_terms, got_ids = tuple(
        (
            part.astype(jnp.float32)
            for part in side_by_side(
                (sent_terms.astype(jnp.bfloat16), sent_ids.astype(jnp.bfloat16)), "narrow", 0, 0, 2
            )
        )
    )
    got_terms = got_terms.reshape(slot_total, block_edges * trip_width)
    got_ids = got_ids.reshape(1, slot_total).astype(jnp.int32)
    selector = (lax.broadcasted_iota(jnp.int32, (local_blocks, 1), 0) == got_ids).astype(
        jnp.bfloat16
    )
    high_part, low_part = split_parts(got_terms)
    source_grad = jnp.dot(selector, high_part, preferred_element_type=jnp.float32) + jnp.dot(
        selector, low_part, preferred_element_type=jnp.float32
    )
    source_grad = source_grad.reshape(local_edges, trip_width)
    grad_pre_down = (source_grad * silu_grad(pre_down)).astype(jnp.bfloat16)
    grad_x = grad_msg + dot_trans(grad_pre_down, down_weight)
    return (output, grad_x.astype(jnp.bfloat16))


def solution(mesh):
    in_specs = (
        P(("cluster", "narrow"), None),
        P(("cluster", "narrow"), None),
        P(),
        P(),
        P(),
        P(),
        P(("cluster", "narrow"), None, None),
        P(("cluster", "narrow")),
        P(("cluster", "narrow"), None),
        P(("cluster", "narrow")),
    )
    out_specs = (P(("cluster", "narrow"), None), P(("cluster", "narrow"), None))
    return jax.shard_map(
        on_device, mesh=mesh, in_specs=in_specs, out_specs=out_specs, check_vma=False
    )
```

```python
import functools
import jax
import jax.numpy as jnp
from jax import lax
from jax.experimental import pallas as pl
from jax.experimental.pallas import tpu as pltpu
from jax.sharding import PartitionSpec as P

CH = 4


def place():
    me = lax.axis_index("narrow")
    core = lax.rem(me, 2)
    far = lax.rem(lax.div(me, 2), 2)
    row = lax.div(me, 4)
    return row, far, core


def slot_of(row, far, core):
    return (lax.rem(row + 4, 4) * 2 + far) * 2 + core


def greet(partners):
    barrier = pltpu.get_barrier_semaphore()
    for p in partners:
        pl.semaphore_signal(
            barrier, inc=1, device_id={"narrow": p}, device_id_type=pl.DeviceIdType.MESH
        )
    pl.semaphore_wait(barrier, len(partners))


def push(src, dst, send, recv, target):
    return pltpu.make_async_remote_copy(
        src_ref=src,
        dst_ref=dst,
        send_sem=send,
        recv_sem=recv,
        device_id={"narrow": target},
        device_id_type=pl.DeviceIdType.MESH,
    )


def gather_kernel(own, out, loc, ysend, yrecv, y2send, y2recv, zsend, zrecv, csend, crecv):
    row, far, core = place()
    up, dn = slot_of(row + 1, far, core), slot_of(row - 1, far, core)
    anti, sib = slot_of(row, 1 - far, core), slot_of(row, far, 1 - core)
    me = slot_of(row, far, core)
    rows = own.shape[0] // CH

    def part(ref, slot, q):
        return ref.at[slot, pl.ds(q * rows, rows)]

    greet((up, dn, anti, sib))
    keep = pltpu.make_async_copy(own, out.at[me], loc)
    keep.start()
    copies = []

    def go(c):
        c.start()
        copies.append(c)
        return c

    zc = [
        go(push(own.at[pl.ds(q * rows, rows)], part(out, me, q), zsend.at[q], zrecv.at[q], anti))
        for q in range(CH)
    ]
    order = {0: (0, 1, 2, 3), 1: (2, 3, 0, 1)}
    half = {0: (0, 1), 1: (2, 3)}
    nbr = (up, dn)
    yc = {}
    for i in range(CH):
        for d in (0, 1):
            q = order[d][i]
            yc[0, d, q] = go(
                push(
                    own.at[pl.ds(q * rows, rows)],
                    part(out, me, q),
                    ysend.at[0, d, q],
                    yrecv.at[0, d, q],
                    nbr[d],
                )
            )
    cc = [go(push(own, out.at[me], csend.at[0], crecv.at[0], sib))]

    def relay(z, d, q):
        yc[z, d, q].wait_recv()
        if q in half[d]:
            came = slot_of(row - 1 if d == 0 else row + 1, far if z == 0 else 1 - far, core)
            y2[z, q] = go(
                push(part(out, came, q), part(out, came, q), y2send.at[z, q], y2recv.at[z, q], nbr[d])
            )

    def to_sib(slot, i):
        cc.append(go(push(out.at[slot], out.at[slot], csend.at[i], crecv.at[i], sib)))

    y2 = {}
    for i in range(CH):
        for d in (0, 1):
            relay(0, d, order[d][i])
    to_sib(dn, 1)
    to_sib(up, 2)
    for q in range(CH):
        zc[q].wait_recv()
        for d in (0, 1):
            yc[1, d, q] = go(
                push(part(out, anti, q), part(out, anti, q), ysend.at[1, d, q], yrecv.at[1, d, q], nbr[d])
            )
    to_sib(anti, 3)
    for q in range(CH):
        y2[0, q].wait_recv()
    to_sib(slot_of(row + 2, far, core), 4)
    for i in range(CH):
        for d in (0, 1):
            relay(1, d, order[d][i])
    to_sib(slot_of(row - 1, 1 - far, core), 5)
    to_sib(slot_of(row + 1, 1 - far, core), 6)
    for q in range(CH):
        y2[1, q].wait_recv()
    to_sib(slot_of(row + 2, 1 - far, core), 7)
    for c in cc:
        c.wait_recv()
    for c in copies:
        c.wait_send()
    keep.wait()


def all_gather(own):
    dma = pltpu.SemaphoreType.DMA
    return pl.pallas_call(
        gather_kernel,
        name="gather_narrow",
        out_shape=jax.ShapeDtypeStruct((16, *own.shape), own.dtype),
        in_specs=[pl.BlockSpec(memory_space=pl.ANY)],
        out_specs=pl.BlockSpec(memory_space=pl.ANY),
        scratch_shapes=[
            dma,
            dma((2, 2, CH)),
            dma((2, 2, CH)),
            dma((2, CH)),
            dma((2, CH)),
            dma((CH,)),
            dma((CH,)),
            dma((8,)),
            dma((8,)),
        ],
        compiler_params=pltpu.CompilerParams(collective_id=0, has_side_effects=True),
    )(own)


def scatter_kernel(parts, out, near_buf, y2buf, ybuf, zbuf, stage, psend, precv, y2send, y2recv, ysend, yrecv, zsend, zrecv):
    row, far, core = place()
    up, dn = slot_of(row + 1, far, core), slot_of(row - 1, far, core)
    anti, sib = slot_of(row, 1 - far, core), slot_of(row, far, 1 - core)
    nbr = (up, dn)
    rows = out.shape[0] // CH
    half = {0: (0, 1), 1: (2, 3)}
    greet((up, dn, anti, sib))
    copies = []

    def go(c):
        c.start()
        copies.append(c)
        return c

    def far_of(z):
        return 1 - far if z == 0 else far

    hops = (2, 1, 3, 0)
    sc = {}
    for z in (0, 1):
        for o in hops:
            dest = slot_of(row + o, far_of(z), 1 - core)
            sc[z, o] = go(
                push(parts.at[dest], near_buf.at[z, o], psend.at[z, o], precv.at[z, o], sib)
            )

    def chip_sum(z, o, q):
        sl = pl.ds(q * rows, rows)
        mine = parts[slot_of(row + o, far_of(z), core), sl].astype(jnp.float32)
        return mine + near_buf[z, o, sl].astype(jnp.float32)

    y2, yc, zc = {}, {}, {}

    def send_y2(z):
        sc[z, 2].wait_recv()
        for d in (0, 1):
            for q in half[d]:
                sl = pl.ds(q * rows, rows)
                stage[z, 2, sl] = chip_sum(z, 2, q).astype(jnp.bfloat16)
                y2[z, q] = go(
                    push(stage.at[z, 2, sl], y2buf.at[z, sl], y2send.at[z, q], y2recv.at[z, q], nbr[d])
                )

    def send_y(z):
        for d, o in ((0, 1), (1, 3)):
            sc[z, o].wait_recv()
        for d, o in ((0, 1), (1, 3)):
            for q in half[1 - d]:
                sl = pl.ds(q * rows, rows)
                stage[z, o, sl] = chip_sum(z, o, q).astype(jnp.bfloat16)
                yc[z, d, q] = go(
                    push(stage.at[z, o, sl], ybuf.at[z, d, sl], ysend.at[z, d, q], yrecv.at[z, d, q], nbr[d])
                )
        for i in (0, 1):
            for d, o in ((0, 1), (1, 3)):
                q = half[d][i]
                sl = pl.ds(q * rows, rows)
                y2[z, q].wait_recv()
                stage[z, o, sl] = (
                    chip_sum(z, o, q) + y2buf[z, sl].astype(jnp.float32)
                ).astype(jnp.bfloat16)
                yc[z, d, q] = go(
                    push(stage.at[z, o, sl], ybuf.at[z, d, sl], ysend.at[z, d, q], yrecv.at[z, d, q], nbr[d])
                )

    def final(z, q):
        sl = pl.ds(q * rows, rows)
        yc[z, 0, q].wait_recv()
        yc[z, 1, q].wait_recv()
        return (
            chip_sum(z, 0, q)
            + ybuf[z, 0, sl].astype(jnp.float32)
            + ybuf[z, 1, sl].astype(jnp.float32)
        )

    send_y2(0)
    send_y(0)
    send_y2(1)
    sc[0, 0].wait_recv()
    for q in (2, 0, 3, 1):
        sl = pl.ds(q * rows, rows)
        stage[0, 0, sl] = final(0, q).astype(jnp.bfloat16)
        zc[q] = go(push(stage.at[0, 0, sl], zbuf.at[sl], zsend.at[q], zrecv.at[q], anti))
    send_y(1)
    sc[1, 0].wait_recv()
    for q in (2, 0, 3, 1):
        sl = pl.ds(q * rows, rows)
        out[sl] = final(1, q)
    for q in (2, 0, 3, 1):
        sl = pl.ds(q * rows, rows)
        zc[q].wait_recv()
        out[sl] = out[sl] + zbuf[sl].astype(jnp.float32)
    for c in copies:
        c.wait_send()


def reduce_scatter(parts):
    dma = pltpu.SemaphoreType.DMA
    n, r, l = parts.shape
    vm = pltpu.VMEM
    return pl.pallas_call(
        scatter_kernel,
        name="scatter_narrow",
        out_shape=jax.ShapeDtypeStruct((r, l), jnp.float32),
        in_specs=[pl.BlockSpec(memory_space=pltpu.VMEM)],
        out_specs=pl.BlockSpec(memory_space=pltpu.VMEM),
        scratch_shapes=[
            vm((2, 4, r, l), jnp.bfloat16),
            vm((2, r, l), jnp.bfloat16),
            vm((2, 2, r, l), jnp.bfloat16),
            vm((r, l), jnp.bfloat16),
            vm((2, 4, r, l), jnp.bfloat16),
            dma((2, 4)),
            dma((2, 4)),
            dma((2, CH)),
            dma((2, CH)),
            dma((2, 2, CH)),
            dma((2, 2, CH)),
            dma((CH,)),
            dma((CH,)),
        ],
        compiler_params=pltpu.CompilerParams(collective_id=1, has_side_effects=True),
    )(parts)


ROOT_HALF = 0.7071067811865476
TILES = 8


def sigmoid(v):
    return 0.5 + 0.5 * jnp.tanh(0.5 * v)


def silu_both(v):
    s = sigmoid(v)
    f = v * s
    return f, s + f * (1.0 - s)


def low_lanes(shape):
    return lax.broadcasted_iota(jnp.int32, shape, len(shape) - 1) < 64


def swap_halves(v):
    return pltpu.roll(v, 64, 1)


def dot(a, b):
    return jnp.dot(a, b, preferred_element_type=jnp.float32)


def dot_rows(a, b):
    return lax.dot_general(a, b, (((1,), (1,)), ((), ())), preferred_element_type=jnp.float32)


def dot_cols(a, b):
    return lax.dot_general(a, b, (((0,), (0,)), ((), ())), preferred_element_type=jnp.float32)


def paired(v):
    n = v.shape[0] // 64
    v = v.reshape(n, 2, 32, 128)
    return jnp.where(low_lanes((n, 32, 128)), v[:, 0], v[:, 1]).reshape(n * 32, 128)


def spread(t):
    n = t.shape[0] // 32
    t = t.reshape(n, 32, 128)
    low = low_lanes(t.shape)
    zero = jnp.zeros_like(t)
    both = jnp.concatenate([jnp.where(low, t, zero), jnp.where(low, zero, t)], axis=1)
    return both.reshape(n * 64, 128)


def pick_rows(rev, table):
    edge = lax.rem(rev, 2048)
    block, rest = lax.div(edge, 64), lax.rem(edge, 64)
    row = block * 32 + lax.rem(rest, 32)
    upper = rest >= 32
    hot = lax.broadcasted_iota(jnp.int32, (rev.shape[0], table.shape[0]), 1) == row
    hot = jnp.where(hot, 1.0, 0.0).astype(jnp.bfloat16)
    got = dot(hot, table)
    return jnp.where(low_lanes(got.shape) != upper, got, 0.0)


def prep_kernel(x, wd2, ang, trip, pre, amat, tmp):
    pair = paired(dot(x[...], wd2[...]))
    pre[...] = pair
    trip[...] = (pair * sigmoid(pair)).astype(jnp.bfloat16)
    low = low_lanes((64, 128))

    def one(k, carry):
        a = ang[k].astype(jnp.float32)
        for r in range(32):
            t = a[:, 128 * r : 128 * r + 128]
            tmp[16 * r : 16 * r + 8] = t
            tmp[16 * r + 8 : 16 * r + 16] = swap_halves(t)
        for s in range(0, 8, 2):
            first = tmp[pl.ds(s, 64, stride=8), :]
            second = tmp[pl.ds(s + 1, 64, stride=8), :]
            both = jnp.where(low, first, swap_halves(second)).astype(jnp.bfloat16)
            amat[pl.ds(pl.multiple_of(k * 64, 64), 64), s * 64 : s * 64 + 128] = both
        return carry

    lax.fori_loop(0, ang.shape[0], one, 0)


def prep(x, wd2, ang):
    n = x.shape[0]
    t = n // TILES
    return pl.pallas_call(
        prep_kernel,
        name="prep",
        grid=(TILES,),
        in_specs=[
            pl.BlockSpec((t, x.shape[1]), lambda i: (i, 0)),
            pl.BlockSpec(wd2.shape, lambda i: (0, 0)),
            pl.BlockSpec((t // 64, 8, 4096), lambda i: (i, 0, 0)),
        ],
        out_specs=[
            pl.BlockSpec((t // 2, 128), lambda i: (i, 0)),
            pl.BlockSpec((t // 2, 128), lambda i: (i, 0)),
            pl.BlockSpec((t, 512), lambda i: (i, 0)),
        ],
        out_shape=[
            jax.ShapeDtypeStruct((n // 2, 128), jnp.bfloat16),
            jax.ShapeDtypeStruct((n // 2, 128), jnp.float32),
            jax.ShapeDtypeStruct((n, 512), jnp.bfloat16),
        ],
        scratch_shapes=[pltpu.VMEM((512, 128), jnp.float32)],
    )(x, wd2, ang)


def blocks_kernel(src, cnt, trips, amat, out, rhs):
    i = pl.program_id(0)
    nk = amat.shape[0] // 64
    for k in range(nk):
        g = i * nk + k
        live = cnt[g]
        for s in range(8):
            b = lax.rem(src[g * 8 + s], 512)
            q = trips[pl.ds(pl.multiple_of(b * 32, 32), 32), :]
            q = jnp.where(s < live, q, jnp.zeros_like(q))
            rhs[k, s * 64 : s * 64 + 32] = q
            rhs[k, s * 64 + 32 : s * 64 + 64] = swap_halves(q)
        o = dot(amat[k * 64 : k * 64 + 64], rhs[k])
        pair = jnp.where(low_lanes((32, 128)), o[:32], swap_halves(o[32:]))
        out[k * 32 : k * 32 + 32] = pair.astype(jnp.bfloat16)


def blocks(src, cnt, trips, amat):
    n = amat.shape[0]
    t = n // TILES
    return pl.pallas_call(
        blocks_kernel,
        name="blocks",
        grid_spec=pltpu.PrefetchScalarGridSpec(
            num_scalar_prefetch=2,
            grid=(TILES,),
            in_specs=[
                pl.BlockSpec(trips.shape, lambda i, *_: (0, 0), pipeline_mode=pl.Buffered(1)),
                pl.BlockSpec((t, 512), lambda i, *_: (i, 0)),
            ],
            out_specs=pl.BlockSpec((t // 2, 128), lambda i, *_: (i, 0)),
            scratch_shapes=[pltpu.VMEM((t // 64, 512, 128), jnp.bfloat16)],
        ),
        out_shape=jax.ShapeDtypeStruct((n // 2, 128), jnp.bfloat16),
    )(src, cnt, trips, amat)


def layer_kernel(x, cot, own, theirs, rev, ww, wi, wo, out, gmsg, hsend, gown):
    c = ROOT_HALF
    w2 = ww[...]
    up, dup = silu_both(dot(spread(own[...]), w2))
    picked = pick_rows(rev[...], theirs[...]).astype(jnp.bfloat16)
    pup, dpup = silu_both(dot(picked, w2))
    up = up.astype(jnp.bfloat16).astype(jnp.float32)
    pup = pup.astype(jnp.bfloat16).astype(jnp.float32)
    hidden = (x[...].astype(jnp.float32) + (up + pup) * c) * c
    act, dact = silu_both(dot(hidden.astype(jnp.bfloat16), wi[...]))
    res, dres = silu_both(dot(act.astype(jnp.bfloat16), wo[...]))
    out[...] = ((hidden + res) * c).astype(jnp.bfloat16)
    scaled = cot[...].astype(jnp.float32) * c
    grad_out = (scaled * dres).astype(jnp.bfloat16)
    grad_in = (dot_rows(grad_out, wo[...]) * dact).astype(jnp.bfloat16)
    grad_msg = (scaled + dot_rows(grad_in, wi[...])) * c
    gmsg[...] = grad_msg
    rounded = grad_msg.astype(jnp.bfloat16).astype(jnp.float32)
    hsend[...] = paired(dot_rows((rounded * (c * dpup)).astype(jnp.bfloat16), w2)).astype(jnp.bfloat16)
    gown[...] = dot_rows((grad_msg * (c * dup)).astype(jnp.bfloat16), w2)


def layer(x, cot, own, theirs, rev, ww, wi, wo):
    n, d = x.shape
    t = n // TILES
    wide = pl.BlockSpec((t, d), lambda i: (i, 0))

    def whole(a):
        return pl.BlockSpec(a.shape, lambda i: (0, 0))

    return pl.pallas_call(
        layer_kernel,
        name="layer",
        grid=(TILES,),
        in_specs=[
            wide,
            wide,
            pl.BlockSpec((t // 2, 128), lambda i: (i, 0)),
            whole(theirs),
            pl.BlockSpec((t, 1), lambda i: (i, 0)),
            whole(ww),
            whole(wi),
            whole(wo),
        ],
        out_specs=[
            wide,
            wide,
            pl.BlockSpec((t // 2, 128), lambda i: (i, 0)),
            pl.BlockSpec((t, 128), lambda i: (i, 0)),
        ],
        out_shape=[
            jax.ShapeDtypeStruct((n, d), jnp.bfloat16),
            jax.ShapeDtypeStruct((n, d), jnp.float32),
            jax.ShapeDtypeStruct((n // 2, 128), jnp.bfloat16),
            jax.ShapeDtypeStruct((n, 128), jnp.float32),
        ],
    )(x, cot, own, theirs, rev, ww, wi, wo)


def terms_kernel(src, cnt, got, rev, gown, amat, out, acc):
    i = pl.program_id(0)
    nk = amat.shape[0] // 64

    @pl.when(i == 0)
    def _():
        acc[...] = jnp.zeros_like(acc)

    theirs = pick_rows(rev[...], got[...])
    grad = (gown[...] + theirs + swap_halves(theirs)).astype(jnp.bfloat16)
    for k in range(nk):
        g = i * nk + k
        o = dot_cols(amat[k * 64 : k * 64 + 64], grad[k * 64 : k * 64 + 64])
        pair = paired(o)
        live = cnt[g]
        for s in range(8):
            b = lax.rem(src[g * 8 + s], 512)

            @pl.when(s < live)
            def _(b=b, s=s, pair=pair):
                acc[pl.ds(pl.multiple_of(b * 32, 32), 32), :] += pair[s * 32 : s * 32 + 32]

    @pl.when(i == TILES - 1)
    def _():
        out[...] = acc[...].astype(jnp.bfloat16)


def terms(src, cnt, got, rev, gown, amat):
    n = amat.shape[0]
    t = n // TILES
    return pl.pallas_call(
        terms_kernel,
        name="terms",
        grid_spec=pltpu.PrefetchScalarGridSpec(
            num_scalar_prefetch=2,
            grid=(TILES,),
            in_specs=[
                pl.BlockSpec(got.shape, lambda i, *_: (0, 0)),
                pl.BlockSpec((t, 1), lambda i, *_: (i, 0)),
                pl.BlockSpec((t, 128), lambda i, *_: (i, 0)),
                pl.BlockSpec((t, 512), lambda i, *_: (i, 0)),
            ],
            out_specs=pl.BlockSpec((16384, 128), lambda i, *_: (0, 0), pipeline_mode=pl.Buffered(1)),
            scratch_shapes=[pltpu.VMEM((16384, 128), jnp.float32)],
        ),
        out_shape=jax.ShapeDtypeStruct((16384, 128), jnp.bfloat16),
    )(src, cnt, got, rev, gown, amat)


def last_kernel(gmsg, total, pre, wd2, out):
    grad = (total[...] * silu_both(pre[...])[1]).astype(jnp.bfloat16)
    out[...] = (gmsg[...] + dot_rows(spread(grad), wd2[...])).astype(jnp.bfloat16)


def last(gmsg, total, pre, wd2):
    n, d = gmsg.shape
    t = n // TILES
    wide = pl.BlockSpec((t, d), lambda i: (i, 0))
    slim = pl.BlockSpec((t // 2, 128), lambda i: (i, 0))
    return pl.pallas_call(
        last_kernel,
        name="last",
        grid=(TILES,),
        in_specs=[wide, slim, slim, pl.BlockSpec(wd2.shape, lambda i: (0, 0))],
        out_specs=wide,
        out_shape=jax.ShapeDtypeStruct((n, d), jnp.bfloat16),
    )(gmsg, total, pre, wd2)


def mirrored(v):
    size = lax.axis_size("cluster")
    return lax.ppermute(v, "cluster", [(i, i ^ (size // 2)) for i in range(size)])


def on_device(x, cot, down, up, inner, outer, ang, reverse, sources, counts):
    wd2 = jnp.concatenate([down, down], axis=1)
    ww = jnp.concatenate([up, up], axis=0)
    src = sources.reshape(-1)
    rev = reverse.reshape(-1, 1)
    trip, pre, amat = prep(x, wd2, ang)
    trips = all_gather(trip).reshape(-1, 128)
    own = blocks(src, counts, trips, amat)
    theirs = mirrored(own)
    out, gmsg, hsend, gown = layer(x, cot, own, theirs, rev, ww, inner[0], outer[0])
    got = mirrored(hsend)
    parts = terms(src, counts, got, rev, gown, amat)
    total = reduce_scatter(parts.reshape(16, -1, 128))
    return out, last(gmsg, total, pre, wd2)


def solution(mesh):
    rows = P(("cluster", "narrow"))
    specs = (rows, rows, P(), P(), P(), P(), rows, rows, rows, rows)
    return jax.shard_map(
        on_device, mesh=mesh, in_specs=specs, out_specs=(rows, rows), check_vma=False
    )
```

```python
import functools
import jax
import jax.numpy as jnp
from jax import lax
from jax.experimental import pallas as pl
from jax.experimental.pallas import tpu as pltpu
from jax.sharding import PartitionSpec as P

CH = 4


def place():
    me = lax.axis_index("narrow")
    core = lax.rem(me, 2)
    far = lax.rem(lax.div(me, 2), 2)
    row = lax.div(me, 4)
    return row, far, core


def slot_of(row, far, core):
    return (lax.rem(row + 4, 4) * 2 + far) * 2 + core


ROOT_HALF = 0.7071067811865476
TILES = 8


def sigmoid(v):
    return 0.5 + 0.5 * jnp.tanh(0.5 * v)


def silu_both(v):
    s = sigmoid(v)
    f = v * s
    return f, s + f * (1.0 - s)


def low_lanes(shape):
    return lax.broadcasted_iota(jnp.int32, shape, len(shape) - 1) < 64


def swap_halves(v):
    return pltpu.roll(v, 64, 1)


def dot(a, b):
    return jnp.dot(a, b, preferred_element_type=jnp.float32)


def dot_rows(a, b):
    return lax.dot_general(a, b, (((1,), (1,)), ((), ())), preferred_element_type=jnp.float32)


def dot_cols(a, b):
    return lax.dot_general(a, b, (((0,), (0,)), ((), ())), preferred_element_type=jnp.float32)


def paired(v):
    n = v.shape[0] // 64
    v = v.reshape(n, 2, 32, 128)
    return jnp.where(low_lanes((n, 32, 128)), v[:, 0], v[:, 1]).reshape(n * 32, 128)


def spread(t):
    n = t.shape[0] // 32
    t = t.reshape(n, 32, 128)
    low = low_lanes(t.shape)
    zero = jnp.zeros_like(t)
    both = jnp.concatenate([jnp.where(low, t, zero), jnp.where(low, zero, t)], axis=1)
    return both.reshape(n * 64, 128)


def pick_rows(rev, table):
    edge = lax.rem(rev, 2048)
    block, rest = lax.div(edge, 64), lax.rem(edge, 64)
    row = block * 32 + lax.rem(rest, 32)
    upper = rest >= 32
    hot = lax.broadcasted_iota(jnp.int32, (rev.shape[0], table.shape[0]), 1) == row
    hot = jnp.where(hot, 1.0, 0.0).astype(jnp.bfloat16)
    got = dot(hot, table)
    return jnp.where(low_lanes(got.shape) != upper, got, 0.0)


EDGE_CHUNK = 512


def mirror_id():
    size = lax.axis_size("cluster")
    return {"cluster": lax.rem(lax.axis_index("cluster") + size // 2, size)}


def narrow_id(slot):
    return {"narrow": slot}


def send(src, dst, send_sem, recv_sem, target):
    return pltpu.make_async_remote_copy(
        src_ref=src,
        dst_ref=dst,
        send_sem=send_sem,
        recv_sem=recv_sem,
        device_id=target,
        device_id_type=pl.DeviceIdType.MESH,
    )


def hello(targets):
    barrier = pltpu.get_barrier_semaphore()
    for t in targets:
        pl.semaphore_signal(barrier, inc=1, device_id=t, device_id_type=pl.DeviceIdType.MESH)
    return lambda: pl.semaphore_wait(barrier, len(targets))


def relayout(ang, amat, tmp, k):
    low = low_lanes((64, 128))
    a = ang[k].astype(jnp.float32)
    for r in range(32):
        t = a[:, 128 * r : 128 * r + 128]
        tmp[16 * r : 16 * r + 8] = t
        tmp[16 * r + 8 : 16 * r + 16] = swap_halves(t)
    for s in range(0, 8, 2):
        first = tmp[pl.ds(s, 64, stride=8), :]
        second = tmp[pl.ds(s + 1, 64, stride=8), :]
        both = jnp.where(low, first, swap_halves(second)).astype(jnp.bfloat16)
        amat[pl.ds(pl.multiple_of(k * 64, 64), 64), s * 64 : s * 64 + 128] = both


def front_kernel(
    src, cnt, x, down, ang,
    mine_out, theirs, pre_out, amat_out,
    xbuf, abuf, trips, amat, pre, mine, rhs, tmp,
    xsem, asem, osem, ysend, yrecv, y2send, y2recv, zsend, zrecv, csend, crecv, msend, mrecv,
):
    row, far, core = place()
    up, dn = slot_of(row + 1, far, core), slot_of(row - 1, far, core)
    anti, sib = slot_of(row, 1 - far, core), slot_of(row, far, 1 - core)
    me = slot_of(row, far, core)
    nbr = (narrow_id(up), narrow_id(dn))
    anti_id, sib_id, mirror = narrow_id(anti), narrow_id(sib), mirror_id()
    group = trips.shape[0] // 16 // CH
    rows = group * 32
    half = {0: (0, 1), 1: (2, 3)}
    wd2 = jnp.concatenate([down[...]] * 2, axis=0)
    loads = []
    for q in range(CH):
        sl = pl.ds(q * 2 * rows, 2 * rows)
        loads.append(pltpu.make_async_copy(x.at[sl], xbuf.at[sl], xsem.at[q]))
        loads[-1].start()
    aload = pltpu.make_async_copy(ang, abuf, asem)
    aload.start()
    arrive = hello((*nbr, anti_id, sib_id, mirror))
    copies = []

    def go(c):
        c.start()
        copies.append(c)
        return c

    def part(slot, q):
        return trips.at[pl.ds((slot * CH + q) * group, group)]

    yc, y2, zc, cc = {}, {}, {}, []
    for q in range(CH):
        loads[q].wait()
        pair = paired(dot_rows(xbuf[q * 2 * rows : (q + 1) * 2 * rows], wd2))
        pre[q * rows : (q + 1) * rows] = pair
        fresh = (pair * sigmoid(pair)).astype(jnp.bfloat16)
        part(me, q)[...] = fresh.reshape(group, 32, 128)
        if q == 0:
            arrive()
        zc[q] = go(send(part(me, q), part(me, q), zsend.at[q], zrecv.at[q], anti_id))
        for d in (0, 1):
            yc[0, d, q] = go(
                send(part(me, q), part(me, q), ysend.at[0, d, q], yrecv.at[0, d, q], nbr[d])
            )
        cc.append(go(send(part(me, q), part(me, q), csend.at[0, q], crecv.at[0, q], sib_id)))
    outs = [pltpu.make_async_copy(pre, pre_out, osem.at[0])]
    outs[0].start()
    aload.wait()
    step = [0]
    blocks_n = amat.shape[0] // 64

    def lay(n):
        lo, hi = step[0], min(step[0] + n, blocks_n)
        step[0] = hi

        def one(k, carry):
            relayout(abuf, amat, tmp, k)
            return carry

        if hi > lo:
            lax.fori_loop(lo, hi, one, 0)

    def came(z, d):
        return slot_of(row - 1 if d == 0 else row + 1, far if z == 0 else 1 - far, core)

    def to_sib(slot, i, q):
        cc.append(go(send(part(slot, q), part(slot, q), csend.at[i, q], crecv.at[i, q], sib_id)))

    def pass_on(z, q):
        for d in (0, 1):
            yc[z, d, q].wait_recv()
            slot = came(z, d)
            if q in half[d]:
                y2[z, q] = go(send(part(slot, q), part(slot, q), y2send.at[z, q], y2recv.at[z, q], nbr[d]))
            to_sib(slot, 1 + z * 4 + d, q)

    def from_far(q):
        zc[q].wait_recv()
        for d in (0, 1):
            yc[1, d, q] = go(
                send(part(anti, q), part(anti, q), ysend.at[1, d, q], yrecv.at[1, d, q], nbr[d])
            )
        to_sib(anti, 3, q)

    def far_row(z, q):
        y2[z, q].wait_recv()
        to_sib(slot_of(row + 2, far if z == 0 else 1 - far, core), 4 if z == 0 else 7, q)

    lay(6)
    pass_on(0, 0)
    lay(4)
    pass_on(0, 1)
    lay(4)
    pass_on(0, 2)
    from_far(0)
    lay(3)
    pass_on(0, 3)
    lay(3)
    from_far(1)
    lay(4)
    far_row(0, 0)
    far_row(0, 2)
    from_far(2)
    lay(4)
    pass_on(1, 0)
    far_row(0, 1)
    far_row(0, 3)
    from_far(3)
    lay(blocks_n)
    outs.append(pltpu.make_async_copy(amat, amat_out, osem.at[1]))
    outs[1].start()
    for q in range(1, CH):
        pass_on(1, q)
    for q in range(CH):
        far_row(1, q)
    for c in cc:
        c.wait_recv()

    per = blocks_n // CH
    mc = []
    for q in range(CH):

        def one(k, carry, q=q):
            used = jnp.broadcast_to(cnt[k], (32, 128))
            for s in range(8):
                v = trips[lax.rem(src[s, k], trips.shape[0])]
                v = jnp.where(used > s, v, jnp.zeros_like(v))
                rhs[s * 64 : s * 64 + 32] = v
                rhs[s * 64 + 32 : s * 64 + 64] = swap_halves(v)
            o = dot(amat[pl.ds(pl.multiple_of(k * 64, 64), 64), :], rhs[...])
            pair = jnp.where(low_lanes((32, 128)), o[:32], swap_halves(o[32:]))
            mine[pl.ds(pl.multiple_of(k * 32, 32), 32), :] = pair.astype(jnp.bfloat16)
            return carry

        lax.fori_loop(q * per, (q + 1) * per, one, 0)
        sl = pl.ds(q * rows, rows)
        mc.append(go(send(mine.at[sl], theirs.at[sl], msend.at[q], mrecv.at[q], mirror)))
    outs.append(pltpu.make_async_copy(mine, mine_out, osem.at[2]))
    outs[2].start()
    for c in mc:
        c.wait_recv()
    for c in copies:
        c.wait_send()
    for c in outs:
        c.wait()


def front(src, cnt, x, down, ang):
    n = x.shape[0]
    dma = pltpu.SemaphoreType.DMA
    vm = pltpu.VMEM
    bf, f32 = jnp.bfloat16, jnp.float32
    anywhere = pl.BlockSpec(memory_space=pl.ANY)
    smem = pl.BlockSpec(memory_space=pltpu.SMEM)
    return pl.pallas_call(
        front_kernel,
        name="front",
        in_specs=[smem, smem, anywhere, pl.BlockSpec(memory_space=vm), anywhere],
        out_specs=[anywhere] * 4,
        out_shape=[
            jax.ShapeDtypeStruct((n // 2, 128), bf),
            jax.ShapeDtypeStruct((n // 2, 128), bf),
            jax.ShapeDtypeStruct((n // 2, 128), f32),
            jax.ShapeDtypeStruct((n, 512), bf),
        ],
        scratch_shapes=[
            vm(x.shape, bf),
            vm(ang.shape, bf),
            vm((n // 4, 32, 128), bf),
            vm((n, 512), bf),
            vm((n // 2, 128), f32),
            vm((n // 2, 128), bf),
            vm((512, 128), bf),
            vm((512, 128), f32),
            dma((CH,)),
            dma,
            dma((3,)),
            dma((2, 2, CH)),
            dma((2, 2, CH)),
            dma((2, CH)),
            dma((2, CH)),
            dma((CH,)),
            dma((CH,)),
            dma((8, CH)),
            dma((8, CH)),
            dma((CH,)),
            dma((CH,)),
        ],
        compiler_params=pltpu.CompilerParams(collective_id=0, has_side_effects=True),
    )(src, cnt, x, down, ang)


def layer_kernel(x, cot, own, theirs, rev, up_w, wi, wo, out, gmsg, got, gown, hs, col, ssem, rsem):
    i = pl.program_id(0)
    mirror = mirror_id()

    @pl.when(i == 0)
    def _():
        hello((mirror,))()
        columns(rev, col)

    c = ROOT_HALF
    w2 = jnp.concatenate([up_w[...]] * 2, axis=0)
    here = pl.ds(pl.multiple_of(i * x.shape[0], x.shape[0]), x.shape[0])
    up, dup = silu_both(dot(spread(own[...]), w2))
    picked = pick_rows(col[here, :], theirs[...]).astype(jnp.bfloat16)
    pup, dpup = silu_both(dot(picked, w2))
    up = up.astype(jnp.bfloat16).astype(jnp.float32)
    pup = pup.astype(jnp.bfloat16).astype(jnp.float32)
    hidden = (x[...].astype(jnp.float32) + (up + pup) * c) * c
    act, dact = silu_both(dot(hidden.astype(jnp.bfloat16), wi[...]))
    res, dres = silu_both(dot(act.astype(jnp.bfloat16), wo[...]))
    out[...] = ((hidden + res) * c).astype(jnp.bfloat16)
    scaled = cot[...].astype(jnp.float32) * c
    grad_out = (scaled * dres).astype(jnp.bfloat16)
    grad_in = (dot_rows(grad_out, wo[...]) * dact).astype(jnp.bfloat16)
    grad_msg = (scaled + dot_rows(grad_in, wi[...])) * c
    gmsg[...] = grad_msg
    rounded = grad_msg.astype(jnp.bfloat16).astype(jnp.float32)
    part = (rounded * (c * dpup)).astype(jnp.bfloat16)
    tile = hs.shape[0] // TILES

    def piece(n):
        sl = pl.ds(pl.multiple_of(n * tile, tile), tile)
        return send(hs.at[sl], got.at[sl], ssem.at[n], rsem.at[n], mirror)

    hs[pl.ds(pl.multiple_of(i * tile, tile), tile), :] = paired(dot_rows(part, w2)).astype(jnp.bfloat16)
    piece(i).start()
    gown[...] = dot_rows((grad_msg * (c * dup)).astype(jnp.bfloat16), w2)

    @pl.when(i == TILES - 1)
    def _():
        for n in range(TILES):
            piece(n).wait()


def layer(x, cot, own, theirs, rev, up, wi, wo):
    n, d = x.shape
    t = n // TILES
    wide = pl.BlockSpec((t, d), lambda i: (i, 0))

    def whole(a):
        return pl.BlockSpec(a.shape, lambda i: (0, 0))

    return pl.pallas_call(
        layer_kernel,
        name="layer",
        grid=(TILES,),
        in_specs=[
            wide,
            wide,
            pl.BlockSpec((t // 2, 128), lambda i: (i, 0)),
            whole(theirs),
            whole(rev),
            whole(up),
            whole(wi),
            whole(wo),
        ],
        out_specs=[
            wide,
            wide,
            pl.BlockSpec(memory_space=pl.ANY),
            pl.BlockSpec((t, 128), lambda i: (i, 0)),
        ],
        out_shape=[
            jax.ShapeDtypeStruct((n, d), jnp.bfloat16),
            jax.ShapeDtypeStruct((n, d), jnp.float32),
            jax.ShapeDtypeStruct((n // 2, 128), jnp.bfloat16),
            jax.ShapeDtypeStruct((n, 128), jnp.float32),
        ],
        scratch_shapes=[
            pltpu.VMEM((n // 2, 128), jnp.bfloat16),
            pltpu.VMEM((n, 1), jnp.int32),
            pltpu.SemaphoreType.DMA((TILES,)),
            pltpu.SemaphoreType.DMA((TILES,)),
        ],
        compiler_params=pltpu.CompilerParams(collective_id=2, has_side_effects=True),
    )(x, cot, own, theirs, rev, up, wi, wo)


def columns(rev, col):
    turned = jnp.transpose(rev[...])
    for j in range(rev.shape[0]):
        col[j * 128 : (j + 1) * 128, :] = turned[:, j : j + 1]


def slot_row(src, cnt):
    slots, n = src.shape
    named = lax.rem(src[...], 512)
    used = lax.broadcasted_iota(jnp.int32, (slots, n), 0) < cnt[...]
    named = jnp.where(used, named, -1).astype(jnp.float32)
    wide = jnp.concatenate([named] * 4, axis=1)
    shape = (slots, 4 * n)
    group = lax.div(lax.broadcasted_iota(jnp.int32, shape, 1), n)
    own = lax.rem(lax.broadcasted_iota(jnp.int32, shape, 0), 4)
    kept = jnp.where(group == own, wide, 0.0)
    halves = [jnp.sum(kept[4 * h : 4 * h + 4], axis=0, keepdims=True) for h in (0, 1)]
    return jnp.concatenate(halves, axis=1)


def back_kernel(
    src, cnt, rev, got, gown, amat,
    out,
    col, pairs, hot, parts, near_buf, y2buf, ybuf, zbuf, stage, acc,
    psend, precv, y2send, y2recv, ysend, yrecv, zsend, zrecv,
):
    row, far, core = place()
    up, dn = slot_of(row + 1, far, core), slot_of(row - 1, far, core)
    anti, sib = slot_of(row, 1 - far, core), slot_of(row, far, 1 - core)
    nbr = (narrow_id(up), narrow_id(dn))
    anti_id, sib_id = narrow_id(anti), narrow_id(sib)
    half = {0: (0, 1), 1: (2, 3)}
    arrive = hello((*nbr, anti_id, sib_id))
    columns(rev, col)

    shape = (512, 256)
    at = lax.broadcasted_iota(jnp.int32, shape, 0)
    named = ((lax.rem(lax.div(at, 32), 4) * 2 + lax.rem(lax.div(at, 128), 2)) * 2 + lax.div(at, 256)) * 32
    named = (named + lax.rem(at, 32)).astype(jnp.float32)
    hot[...] = jnp.where(named == slot_row(src, cnt), 1.0, 0.0).astype(jnp.bfloat16)
    tile = 256

    def tiles(i, carry):
        sl = pl.ds(pl.multiple_of(i * tile, tile), tile)
        theirs = pick_rows(col[sl, :], got[...])
        grad = (gown[sl, :] + theirs + swap_halves(theirs)).astype(jnp.bfloat16)
        for k in range(tile // 64):
            a = amat[pl.ds(pl.multiple_of(i * tile + k * 64, 64), 64), :]
            pair = paired(dot_cols(a, grad[k * 64 : k * 64 + 64]))
            for s in range(8):
                to = pl.multiple_of((s * 32 + i * 4 + k) * 32, 32)
                pairs[pl.ds(to, 32), :] = pair[s * 32 : s * 32 + 32]
        return carry

    lax.fori_loop(0, gown.shape[0] // tile, tiles, 0)
    copies = []

    def go(c):
        c.start()
        copies.append(c)
        return c

    sc, y2, yc, zc = {}, {}, {}, {}
    far_of = (1 - far, far)
    bf = jnp.bfloat16

    def build(q):
        def one(r, carry):
            t = pairs[pl.ds(r, 256, stride=32), :].astype(bf)
            parts[r] = dot(hot[...], t).astype(bf)
            return carry

        lax.fori_loop(8 * q, 8 * q + 8, one, 0)
        sl = pl.ds(8 * q, 8)
        mate = pl.ds(pl.multiple_of((1 - core) * 256, 256), 256)
        sc[q] = go(send(parts.at[sl, mate], near_buf.at[sl], psend.at[q], precv.at[q], sib_id))

    def chip_sum(z, o, q):
        sl = pl.ds(8 * q, 8)
        to = far_of[z] * 128 + lax.rem(row + o, 4) * 32
        a = parts[sl, pl.ds(pl.multiple_of(core * 256 + to, 32), 32), :]
        b = near_buf[sl, pl.ds(pl.multiple_of(to, 32), 32), :]
        return a.astype(jnp.float32) + b.astype(jnp.float32)

    def first(z, q):
        sl = pl.ds(8 * q, 8)
        d = 0 if q in half[0] else 1
        stage[z, 2, sl] = chip_sum(z, 2, q).astype(bf)
        y2[z, q] = go(send(stage.at[z, 2, sl], y2buf.at[z, sl], y2send.at[z, q], y2recv.at[z, q], nbr[d]))
        e = 1 - d
        o = 1 if e == 0 else 3
        stage[z, o, sl] = chip_sum(z, o, q).astype(bf)
        yc[z, e, q] = go(send(stage.at[z, o, sl], ybuf.at[z, e, sl], ysend.at[z, e, q], yrecv.at[z, e, q], nbr[e]))

    def second(z, q):
        sl = pl.ds(8 * q, 8)
        d = 0 if q in half[0] else 1
        o = 1 if d == 0 else 3
        y2[z, q].wait_recv()
        stage[z, o, sl] = (chip_sum(z, o, q) + y2buf[z, sl].astype(jnp.float32)).astype(bf)
        yc[z, d, q] = go(send(stage.at[z, o, sl], ybuf.at[z, d, sl], ysend.at[z, d, q], yrecv.at[z, d, q], nbr[d]))

    def final(z, q):
        sl = pl.ds(8 * q, 8)
        yc[z, 0, q].wait_recv()
        yc[z, 1, q].wait_recv()
        return (
            chip_sum(z, 0, q)
            + ybuf[z, 0, sl].astype(jnp.float32)
            + ybuf[z, 1, sl].astype(jnp.float32)
        )

    order = (0, 2, 1, 3)
    arrive()
    build(order[0])
    for i in range(CH):
        if i + 1 < CH:
            build(order[i + 1])
        sc[order[i]].wait_recv()
        first(0, order[i])
    for q in order:
        second(0, q)
        first(1, q)
    for q in order:
        sl = pl.ds(8 * q, 8)
        stage[0, 0, sl] = final(0, q).astype(bf)
        zc[q] = go(send(stage.at[0, 0, sl], zbuf.at[sl], zsend.at[q], zrecv.at[q], anti_id))
        second(1, q)
    for q in order:
        acc[pl.ds(8 * q, 8)] = final(1, q)
    for q in order:
        sl = pl.ds(8 * q, 8)
        zc[q].wait_recv()
        total = acc[sl] + zbuf[sl].astype(jnp.float32)
        for r in range(8):
            out[pl.ds(8 * q + r, 32, stride=32), :] = total[r]
    for c in copies:
        c.wait_send()


def back(src, cnt, rev, got, gown, amat):
    dma = pltpu.SemaphoreType.DMA
    vm = pltpu.VMEM
    bf, f32 = jnp.bfloat16, jnp.float32
    inside = pl.BlockSpec(memory_space=vm)
    return pl.pallas_call(
        back_kernel,
        name="back",
        in_specs=[inside] * 6,
        out_specs=inside,
        out_shape=jax.ShapeDtypeStruct((1024, 128), f32),
        scratch_shapes=[
            vm((2048, 1), jnp.int32),
            vm((8192, 128), f32),
            vm((512, 256), bf),
            vm((32, 512, 128), bf),
            vm((32, 256, 128), bf),
            vm((2, 32, 32, 128), bf),
            vm((2, 2, 32, 32, 128), bf),
            vm((32, 32, 128), bf),
            vm((2, 4, 32, 32, 128), bf),
            vm((32, 32, 128), f32),
            dma((CH,)),
            dma((CH,)),
            dma((2, CH)),
            dma((2, CH)),
            dma((2, 2, CH)),
            dma((2, 2, CH)),
            dma((CH,)),
            dma((CH,)),
        ],
        compiler_params=pltpu.CompilerParams(collective_id=1, has_side_effects=True),
    )(src, cnt, rev, got, gown, amat)


def last_kernel(gmsg, total, pre, down, res, out, res_out):
    res_out[...] = res[...]
    grad = (total[...] * silu_both(pre[...])[1]).astype(jnp.bfloat16)
    w = jnp.concatenate([down[...]] * 2, axis=0)
    out[...] = (gmsg[...] + dot(spread(grad), w)).astype(jnp.bfloat16)


def last(gmsg, total, pre, down, res):
    n, d = gmsg.shape
    t = n // TILES
    wide = pl.BlockSpec((t, d), lambda i: (i, 0))
    slim = pl.BlockSpec((t // 2, 128), lambda i: (i, 0))
    return pl.pallas_call(
        last_kernel,
        name="last",
        grid=(TILES,),
        in_specs=[wide, slim, slim, pl.BlockSpec(down.shape, lambda i: (0, 0)), wide],
        out_specs=[wide, wide],
        out_shape=[jax.ShapeDtypeStruct((n, d), jnp.bfloat16)] * 2,
    )(gmsg, total, pre, down, res)


def on_device(x, cot, down, up, inner, outer, ang, reverse, sources, counts):
    down, src = down.T, sources.T
    rev = reverse.reshape(-1, 128)
    own, theirs, pre, amat = front(src, counts, x, down, ang)
    res, gmsg, got, gown = layer(x, cot, own, theirs, rev, up, inner[0], outer[0])
    total = back(src, counts.reshape(1, -1), rev, got, gown, amat)
    grad_x, out = last(gmsg, total, pre, down, res)
    return out, grad_x


def solution(mesh):
    rows = P(("cluster", "narrow"))
    specs = (rows, rows, P(), P(), P(), P(), rows, rows, rows, rows)
    return jax.shard_map(
        on_device, mesh=mesh, in_specs=specs, out_specs=(rows, rows), check_vma=False
    )
```

```python
import functools
import jax
import jax.numpy as jnp
from jax import lax
from jax.experimental import pallas as pl
from jax.experimental.pallas import tpu as pltpu
from jax.sharding import PartitionSpec as P

CH = 4


def place():
    me = lax.axis_index("narrow")
    core = lax.rem(me, 2)
    far = lax.rem(lax.div(me, 2), 2)
    row = lax.div(me, 4)
    return row, far, core


def slot_of(row, far, core):
    return (lax.rem(row + 4, 4) * 2 + far) * 2 + core


ROOT_HALF = 0.7071067811865476
TILES = 8
LAST_TILES = 4


def sigmoid(v):
    return 0.5 + 0.5 * jnp.tanh(0.5 * v)


def silu_both(v):
    s = sigmoid(v)
    f = v * s
    return f, s + f * (1.0 - s)


def low_lanes(shape):
    return lax.broadcasted_iota(jnp.int32, shape, len(shape) - 1) < 64


def swap_halves(v):
    return pltpu.roll(v, 64, 1)


def dot(a, b):
    return jnp.dot(a, b, preferred_element_type=jnp.float32)


def dot_rows(a, b):
    return lax.dot_general(a, b, (((1,), (1,)), ((), ())), preferred_element_type=jnp.float32)


def dot_cols(a, b):
    return lax.dot_general(a, b, (((0,), (0,)), ((), ())), preferred_element_type=jnp.float32)


def paired(v):
    n = v.shape[0] // 64
    v = v.reshape(n, 2, 32, 128)
    return jnp.where(low_lanes((n, 32, 128)), v[:, 0], v[:, 1]).reshape(n * 32, 128)


def spread(t):
    n = t.shape[0] // 32
    t = t.reshape(n, 32, 128)
    low = low_lanes(t.shape)
    zero = jnp.zeros_like(t)
    both = jnp.concatenate([jnp.where(low, t, zero), jnp.where(low, zero, t)], axis=1)
    return both.reshape(n * 64, 128)


def pick_rows(rev, table):
    edge = lax.rem(rev, 2048)
    block, rest = lax.div(edge, 64), lax.rem(edge, 64)
    row = block * 32 + lax.rem(rest, 32)
    upper = rest >= 32
    hot = lax.broadcasted_iota(jnp.int32, (rev.shape[0], table.shape[0]), 1) == row
    hot = jnp.where(hot, 1.0, 0.0).astype(jnp.bfloat16)
    got = dot(hot, table)
    return jnp.where(low_lanes(got.shape) != upper, got, 0.0)


EDGE_CHUNK = 512


def mirror_id():
    size = lax.axis_size("cluster")
    return {"cluster": lax.rem(lax.axis_index("cluster") + size // 2, size)}


def narrow_id(slot):
    return {"narrow": slot}


def send(src, dst, send_sem, recv_sem, target):
    return pltpu.make_async_remote_copy(
        src_ref=src,
        dst_ref=dst,
        send_sem=send_sem,
        recv_sem=recv_sem,
        device_id=target,
        device_id_type=pl.DeviceIdType.MESH,
    )


def hello(targets):
    barrier = pltpu.get_barrier_semaphore()
    for t in targets:
        pl.semaphore_signal(barrier, inc=1, device_id=t, device_id_type=pl.DeviceIdType.MESH)
    return lambda: pl.semaphore_wait(barrier, len(targets))


def relayout(ang, amat, tmp, k):
    low = low_lanes((64, 128))
    a = ang[k].astype(jnp.float32)
    for r in range(32):
        t = a[:, 128 * r : 128 * r + 128]
        tmp[16 * r : 16 * r + 8] = t
        tmp[16 * r + 8 : 16 * r + 16] = swap_halves(t)
    for s in range(0, 8, 2):
        first = tmp[pl.ds(s, 64, stride=8), :]
        second = tmp[pl.ds(s + 1, 64, stride=8), :]
        both = jnp.where(low, first, swap_halves(second)).astype(jnp.bfloat16)
        amat[pl.ds(pl.multiple_of(k * 64, 64), 64), s * 64 : s * 64 + 128] = both


def front_kernel(
    src, cnt, x, down, up_w, ang,
    theirs, pre_out, amat_out, up_out, slope_out,
    xbuf, abuf, trips, amat, pre, mine, rhs, tmp, ups, slopes,
    xsem, asem, osem, usem, ysend, yrecv, y2send, y2recv, zsend, zrecv, csend, crecv, msend, mrecv,
):
    row, far, core = place()
    up, dn = slot_of(row + 1, far, core), slot_of(row - 1, far, core)
    anti, sib = slot_of(row, 1 - far, core), slot_of(row, far, 1 - core)
    me = slot_of(row, far, core)
    nbr = (narrow_id(up), narrow_id(dn))
    anti_id, sib_id, mirror = narrow_id(anti), narrow_id(sib), mirror_id()
    group = trips.shape[0] // 16 // CH
    rows = group * 32
    half = {0: (0, 1), 1: (2, 3)}
    wd2 = jnp.concatenate([down[...]] * 2, axis=0)
    loads = []
    for q in range(CH):
        sl = pl.ds(q * 2 * rows, 2 * rows)
        loads.append(pltpu.make_async_copy(x.at[sl], xbuf.at[sl], xsem.at[q]))
        loads[-1].start()
    aload = pltpu.make_async_copy(ang, abuf, asem)
    aload.start()
    arrive = hello((*nbr, anti_id, sib_id, mirror))
    copies = []

    def go(c):
        c.start()
        copies.append(c)
        return c

    def part(slot, q):
        return trips.at[pl.ds((slot * CH + q) * group, group)]

    yc, y2, zc, cc = {}, {}, {}, []
    for q in range(CH):
        loads[q].wait()
        pair = paired(dot_rows(xbuf[q * 2 * rows : (q + 1) * 2 * rows], wd2))
        pre[q * rows : (q + 1) * rows] = pair
        fresh = (pair * sigmoid(pair)).astype(jnp.bfloat16)
        part(me, q)[...] = fresh.reshape(group, 32, 128)
        if q == 0:
            arrive()
        zc[q] = go(send(part(me, q), part(me, q), zsend.at[q], zrecv.at[q], anti_id))
        for d in (0, 1):
            yc[0, d, q] = go(
                send(part(me, q), part(me, q), ysend.at[0, d, q], yrecv.at[0, d, q], nbr[d])
            )
        cc.append(go(send(part(me, q), part(me, q), csend.at[0, q], crecv.at[0, q], sib_id)))
    outs = [pltpu.make_async_copy(pre, pre_out, osem.at[0])]
    outs[0].start()
    aload.wait()
    step = [0]
    blocks_n = amat.shape[0] // 64

    def lay(n):
        lo, hi = step[0], min(step[0] + n, blocks_n)
        step[0] = hi

        def one(k, carry):
            relayout(abuf, amat, tmp, k)
            return carry

        if hi > lo:
            lax.fori_loop(lo, hi, one, 0)

    def came(z, d):
        return slot_of(row - 1 if d == 0 else row + 1, far if z == 0 else 1 - far, core)

    def to_sib(slot, i, q):
        cc.append(go(send(part(slot, q), part(slot, q), csend.at[i, q], crecv.at[i, q], sib_id)))

    def pass_on(z, q):
        for d in (0, 1):
            yc[z, d, q].wait_recv()
            slot = came(z, d)
            if q in half[d]:
                y2[z, q] = go(send(part(slot, q), part(slot, q), y2send.at[z, q], y2recv.at[z, q], nbr[d]))
            to_sib(slot, 1 + z * 4 + d, q)

    def from_far(q):
        zc[q].wait_recv()
        for d in (0, 1):
            yc[1, d, q] = go(
                send(part(anti, q), part(anti, q), ysend.at[1, d, q], yrecv.at[1, d, q], nbr[d])
            )
        to_sib(anti, 3, q)

    def far_row(z, q):
        y2[z, q].wait_recv()
        to_sib(slot_of(row + 2, far if z == 0 else 1 - far, core), 4 if z == 0 else 7, q)

    lay(6)
    pass_on(0, 0)
    lay(4)
    pass_on(0, 1)
    lay(4)
    pass_on(0, 2)
    from_far(0)
    lay(3)
    pass_on(0, 3)
    lay(3)
    from_far(1)
    lay(4)
    far_row(0, 0)
    far_row(0, 2)
    from_far(2)
    lay(4)
    pass_on(1, 0)
    far_row(0, 1)
    far_row(0, 3)
    from_far(3)
    lay(blocks_n)
    outs.append(pltpu.make_async_copy(amat, amat_out, osem.at[1]))
    outs[1].start()
    for q in range(1, CH):
        pass_on(1, q)
    for q in range(CH):
        far_row(1, q)
    for c in cc:
        c.wait_recv()

    per = blocks_n // CH
    mc = []
    for q in range(CH):

        def one(k, carry, q=q):
            used = jnp.broadcast_to(cnt[k], (32, 128))
            for s in range(8):
                v = trips[lax.rem(src[s, k], trips.shape[0])]
                v = jnp.where(used > s, v, jnp.zeros_like(v))
                rhs[s * 64 : s * 64 + 32] = v
                rhs[s * 64 + 32 : s * 64 + 64] = swap_halves(v)
            o = dot(amat[pl.ds(pl.multiple_of(k * 64, 64), 64), :], rhs[...])
            pair = jnp.where(low_lanes((32, 128)), o[:32], swap_halves(o[32:]))
            mine[pl.ds(pl.multiple_of(k * 32, 32), 32), :] = pair.astype(jnp.bfloat16)
            return carry

        lax.fori_loop(q * per, (q + 1) * per, one, 0)
        sl = pl.ds(q * rows, rows)
        mc.append(go(send(mine.at[sl], theirs.at[sl], msend.at[q], mrecv.at[q], mirror)))
    w2 = jnp.concatenate([up_w[...]] * 2, axis=0)
    for q in range(CH):

        def raise_tile(i, carry):
            own = mine[pl.ds(pl.multiple_of(i * 128, 128), 128), :]
            value, slope = silu_both(dot(spread(own), w2))
            sl = pl.ds(pl.multiple_of(i * 256, 256), 256)
            ups[sl, :] = value.astype(jnp.bfloat16)
            slopes[sl, :] = slope.astype(jnp.bfloat16)
            return carry

        lax.fori_loop(q * rows // 128, (q + 1) * rows // 128, raise_tile, 0)
        sl = pl.ds(q * 2 * rows, 2 * rows)
        for j, (a, b) in enumerate(((ups, up_out), (slopes, slope_out))):
            outs.append(pltpu.make_async_copy(a.at[sl], b.at[sl], usem.at[j, q]))
            outs[-1].start()
    for c in mc:
        c.wait_recv()
    for c in copies:
        c.wait_send()
    for c in outs:
        c.wait()


def front(src, cnt, x, down, up, ang):
    n = x.shape[0]
    dma = pltpu.SemaphoreType.DMA
    vm = pltpu.VMEM
    bf, f32 = jnp.bfloat16, jnp.float32
    anywhere = pl.BlockSpec(memory_space=pl.ANY)
    smem = pl.BlockSpec(memory_space=pltpu.SMEM)
    return pl.pallas_call(
        front_kernel,
        name="front",
        in_specs=[smem, smem, anywhere] + [pl.BlockSpec(memory_space=vm)] * 2 + [anywhere],
        out_specs=[anywhere] * 5,
        out_shape=[
            jax.ShapeDtypeStruct((n // 2, 128), bf),
            jax.ShapeDtypeStruct((n // 2, 128), f32),
            jax.ShapeDtypeStruct((n, 512), bf),
            jax.ShapeDtypeStruct((n, 512), bf),
            jax.ShapeDtypeStruct((n, 512), bf),
        ],
        scratch_shapes=[
            vm(x.shape, bf),
            vm(ang.shape, bf),
            vm((n // 4, 32, 128), bf),
            vm((n, 512), bf),
            vm((n // 2, 128), f32),
            vm((n // 2, 128), bf),
            vm((512, 128), bf),
            vm((512, 128), f32),
            vm((n, 512), bf),
            vm((n, 512), bf),
            dma((CH,)),
            dma,
            dma((2,)),
            dma((2, CH)),
            dma((2, 2, CH)),
            dma((2, 2, CH)),
            dma((2, CH)),
            dma((2, CH)),
            dma((CH,)),
            dma((CH,)),
            dma((8, CH)),
            dma((8, CH)),
            dma((CH,)),
            dma((CH,)),
        ],
        compiler_params=pltpu.CompilerParams(collective_id=0, has_side_effects=True),
    )(src, cnt, x, down, up, ang)


def layer_kernel(x, cot, ups, slopes, theirs, rev, up_w, wi, wo, out, gmsg, got, gown, hs, col, ssem, rsem):
    i = pl.program_id(0)
    mirror = mirror_id()

    @pl.when(i == 0)
    def _():
        hello((mirror,))()
        columns(rev, col)

    c = ROOT_HALF
    w2 = jnp.concatenate([up_w[...]] * 2, axis=0)
    here = pl.ds(pl.multiple_of(i * x.shape[0], x.shape[0]), x.shape[0])
    up, dup = ups[...].astype(jnp.float32), slopes[...].astype(jnp.float32)
    picked = pick_rows(col[here, :], theirs[...]).astype(jnp.bfloat16)
    pup, dpup = silu_both(dot(picked, w2))
    pup = pup.astype(jnp.bfloat16).astype(jnp.float32)
    hidden = (x[...].astype(jnp.float32) + (up + pup) * c) * c
    act, dact = silu_both(dot(hidden.astype(jnp.bfloat16), wi[...]))
    res, dres = silu_both(dot(act.astype(jnp.bfloat16), wo[...]))
    out[...] = ((hidden + res) * c).astype(jnp.bfloat16)
    scaled = cot[...].astype(jnp.float32) * c
    grad_out = (scaled * dres).astype(jnp.bfloat16)
    grad_in = (dot_rows(grad_out, wo[...]) * dact).astype(jnp.bfloat16)
    grad_msg = (scaled + dot_rows(grad_in, wi[...])) * c
    gmsg[...] = grad_msg.astype(jnp.bfloat16)
    rounded = grad_msg.astype(jnp.bfloat16).astype(jnp.float32)
    part = (rounded * (c * dpup)).astype(jnp.bfloat16)
    tile = hs.shape[0] // TILES

    def piece(n):
        sl = pl.ds(pl.multiple_of(n * tile, tile), tile)
        return send(hs.at[sl], got.at[sl], ssem.at[n], rsem.at[n], mirror)

    hs[pl.ds(pl.multiple_of(i * tile, tile), tile), :] = paired(dot_rows(part, w2)).astype(jnp.bfloat16)
    piece(i).start()
    gown[...] = dot_rows((grad_msg * (c * dup)).astype(jnp.bfloat16), w2)

    @pl.when(i == TILES - 1)
    def _():
        for n in range(TILES):
            piece(n).wait()


def layer(x, cot, ups, slopes, theirs, rev, up, wi, wo):
    n, d = x.shape
    t = n // TILES
    wide = pl.BlockSpec((t, d), lambda i: (i, 0))

    def whole(a):
        return pl.BlockSpec(a.shape, lambda i: (0, 0))

    return pl.pallas_call(
        layer_kernel,
        name="layer",
        grid=(TILES,),
        in_specs=[
            wide,
            wide,
            wide,
            wide,
            whole(theirs),
            whole(rev),
            whole(up),
            whole(wi),
            whole(wo),
        ],
        out_specs=[
            wide,
            wide,
            pl.BlockSpec(memory_space=pl.ANY),
            pl.BlockSpec((t, 128), lambda i: (i, 0)),
        ],
        out_shape=[
            jax.ShapeDtypeStruct((n, d), jnp.bfloat16),
            jax.ShapeDtypeStruct((n, d), jnp.bfloat16),
            jax.ShapeDtypeStruct((n // 2, 128), jnp.bfloat16),
            jax.ShapeDtypeStruct((n, 128), jnp.float32),
        ],
        scratch_shapes=[
            pltpu.VMEM((n // 2, 128), jnp.bfloat16),
            pltpu.VMEM((n, 1), jnp.int32),
            pltpu.SemaphoreType.DMA((TILES,)),
            pltpu.SemaphoreType.DMA((TILES,)),
        ],
        compiler_params=pltpu.CompilerParams(collective_id=2, has_side_effects=True),
    )(x, cot, ups, slopes, theirs, rev, up, wi, wo)


def columns(rev, col):
    turned = jnp.transpose(rev[...])
    for j in range(rev.shape[0]):
        col[j * 128 : (j + 1) * 128, :] = turned[:, j : j + 1]


def slot_row(src, cnt):
    slots, n = src.shape
    named = lax.rem(src[...], 512)
    used = lax.broadcasted_iota(jnp.int32, (slots, n), 0) < cnt[...]
    named = jnp.where(used, named, -1).astype(jnp.float32)
    wide = jnp.concatenate([named] * 4, axis=1)
    shape = (slots, 4 * n)
    group = lax.div(lax.broadcasted_iota(jnp.int32, shape, 1), n)
    own = lax.rem(lax.broadcasted_iota(jnp.int32, shape, 0), 4)
    kept = jnp.where(group == own, wide, 0.0)
    halves = [jnp.sum(kept[4 * h : 4 * h + 4], axis=0, keepdims=True) for h in (0, 1)]
    return jnp.concatenate(halves, axis=1)


def back_kernel(
    src, cnt, rev, got, gown, amat,
    out,
    col, pairs, hot, parts, near_buf, y2buf, ybuf, zbuf, stage, acc,
    psend, precv, y2send, y2recv, ysend, yrecv, zsend, zrecv,
):
    row, far, core = place()
    up, dn = slot_of(row + 1, far, core), slot_of(row - 1, far, core)
    anti, sib = slot_of(row, 1 - far, core), slot_of(row, far, 1 - core)
    nbr = (narrow_id(up), narrow_id(dn))
    anti_id, sib_id = narrow_id(anti), narrow_id(sib)
    half = {0: (0, 1), 1: (2, 3)}
    arrive = hello((*nbr, anti_id, sib_id))
    columns(rev, col)

    shape = (512, 256)
    at = lax.broadcasted_iota(jnp.int32, shape, 0)
    named = ((lax.rem(lax.div(at, 32), 4) * 2 + lax.rem(lax.div(at, 128), 2)) * 2 + lax.div(at, 256)) * 32
    named = (named + lax.rem(at, 32)).astype(jnp.float32)
    hot[...] = jnp.where(named == slot_row(src, cnt), 1.0, 0.0).astype(jnp.bfloat16)
    tile = 256

    def tiles(i, carry):
        sl = pl.ds(pl.multiple_of(i * tile, tile), tile)
        theirs = pick_rows(col[sl, :], got[...])
        grad = (gown[sl, :] + theirs + swap_halves(theirs)).astype(jnp.bfloat16)
        for k in range(tile // 64):
            a = amat[pl.ds(pl.multiple_of(i * tile + k * 64, 64), 64), :]
            pair = paired(dot_cols(a, grad[k * 64 : k * 64 + 64]))
            for s in range(8):
                to = pl.multiple_of((s * 32 + i * 4 + k) * 32, 32)
                pairs[pl.ds(to, 32), :] = pair[s * 32 : s * 32 + 32]
        return carry

    lax.fori_loop(0, gown.shape[0] // tile, tiles, 0)
    copies = []

    def go(c):
        c.start()
        copies.append(c)
        return c

    sc, y2, yc, zc = {}, {}, {}, {}
    far_of = (1 - far, far)
    bf = jnp.bfloat16

    def build(q):
        def one(g, carry):
            t = [pairs[pl.ds(g * 2 + e, 256, stride=32), :].astype(bf) for e in (0, 1)]
            both = dot(hot[...], jnp.concatenate(t, axis=1)).astype(bf)
            for e in (0, 1):
                parts[g * 2 + e] = both[:, e * 128 : e * 128 + 128]
            return carry

        lax.fori_loop(4 * q, 4 * q + 4, one, 0)
        sl = pl.ds(8 * q, 8)
        mate = pl.ds(pl.multiple_of((1 - core) * 256, 256), 256)
        sc[q] = go(send(parts.at[sl, mate], near_buf.at[sl], psend.at[q], precv.at[q], sib_id))

    def chip_sum(z, o, q):
        sl = pl.ds(8 * q, 8)
        to = far_of[z] * 128 + lax.rem(row + o, 4) * 32
        a = parts[sl, pl.ds(pl.multiple_of(core * 256 + to, 32), 32), :]
        b = near_buf[sl, pl.ds(pl.multiple_of(to, 32), 32), :]
        return a.astype(jnp.float32) + b.astype(jnp.float32)

    def first(z, q):
        sl = pl.ds(8 * q, 8)
        d = 0 if q in half[0] else 1
        stage[z, 2, sl] = chip_sum(z, 2, q).astype(bf)
        y2[z, q] = go(send(stage.at[z, 2, sl], y2buf.at[z, sl], y2send.at[z, q], y2recv.at[z, q], nbr[d]))
        e = 1 - d
        o = 1 if e == 0 else 3
        stage[z, o, sl] = chip_sum(z, o, q).astype(bf)
        yc[z, e, q] = go(send(stage.at[z, o, sl], ybuf.at[z, e, sl], ysend.at[z, e, q], yrecv.at[z, e, q], nbr[e]))

    def second(z, q):
        sl = pl.ds(8 * q, 8)
        d = 0 if q in half[0] else 1
        o = 1 if d == 0 else 3
        y2[z, q].wait_recv()
        stage[z, o, sl] = (chip_sum(z, o, q) + y2buf[z, sl].astype(jnp.float32)).astype(bf)
        yc[z, d, q] = go(send(stage.at[z, o, sl], ybuf.at[z, d, sl], ysend.at[z, d, q], yrecv.at[z, d, q], nbr[d]))

    def final(z, q):
        sl = pl.ds(8 * q, 8)
        yc[z, 0, q].wait_recv()
        yc[z, 1, q].wait_recv()
        return (
            chip_sum(z, 0, q)
            + ybuf[z, 0, sl].astype(jnp.float32)
            + ybuf[z, 1, sl].astype(jnp.float32)
        )

    order = (0, 2, 1, 3)
    arrive()
    build(order[0])
    for i in range(CH):
        if i + 1 < CH:
            build(order[i + 1])
        sc[order[i]].wait_recv()
        first(0, order[i])
    for q in order:
        second(0, q)
        first(1, q)
    for q in order:
        sl = pl.ds(8 * q, 8)
        stage[0, 0, sl] = final(0, q).astype(bf)
        zc[q] = go(send(stage.at[0, 0, sl], zbuf.at[sl], zsend.at[q], zrecv.at[q], anti_id))
        second(1, q)
    for q in order:
        acc[pl.ds(8 * q, 8)] = final(1, q)
    for q in order:
        sl = pl.ds(8 * q, 8)
        zc[q].wait_recv()
        total = acc[sl] + zbuf[sl].astype(jnp.float32)
        for r in range(8):
            out[pl.ds(8 * q + r, 32, stride=32), :] = total[r]
    for c in copies:
        c.wait_send()


def back(src, cnt, rev, got, gown, amat):
    dma = pltpu.SemaphoreType.DMA
    vm = pltpu.VMEM
    bf, f32 = jnp.bfloat16, jnp.float32
    inside = pl.BlockSpec(memory_space=vm)
    return pl.pallas_call(
        back_kernel,
        name="back",
        in_specs=[inside] * 6,
        out_specs=inside,
        out_shape=jax.ShapeDtypeStruct((1024, 128), f32),
        scratch_shapes=[
            vm((2048, 1), jnp.int32),
            vm((8192, 128), f32),
            vm((512, 256), bf),
            vm((32, 512, 128), bf),
            vm((32, 256, 128), bf),
            vm((2, 32, 32, 128), bf),
            vm((2, 2, 32, 32, 128), bf),
            vm((32, 32, 128), bf),
            vm((2, 4, 32, 32, 128), bf),
            vm((32, 32, 128), f32),
            dma((CH,)),
            dma((CH,)),
            dma((2, CH)),
            dma((2, CH)),
            dma((2, 2, CH)),
            dma((2, 2, CH)),
            dma((CH,)),
            dma((CH,)),
        ],
        compiler_params=pltpu.CompilerParams(collective_id=1, has_side_effects=True),
    )(src, cnt, rev, got, gown, amat)


def last_kernel(gmsg, total, pre, down, res, out, res_out):
    res_out[...] = res[...]
    grad = (total[...] * silu_both(pre[...])[1]).astype(jnp.bfloat16)
    w = jnp.concatenate([down[...]] * 2, axis=0)
    out[...] = (gmsg[...].astype(jnp.float32) + dot(spread(grad), w)).astype(jnp.bfloat16)


def last(gmsg, total, pre, down, res):
    n, d = gmsg.shape
    t = n // LAST_TILES
    wide = pl.BlockSpec((t, d), lambda i: (i, 0))
    slim = pl.BlockSpec((t // 2, 128), lambda i: (i, 0))
    return pl.pallas_call(
        last_kernel,
        name="last",
        grid=(LAST_TILES,),
        in_specs=[wide, slim, slim, pl.BlockSpec(down.shape, lambda i: (0, 0)), wide],
        out_specs=[wide, wide],
        out_shape=[jax.ShapeDtypeStruct((n, d), jnp.bfloat16)] * 2,
    )(gmsg, total, pre, down, res)


def on_device(x, cot, down, up, inner, outer, ang, reverse, sources, counts):
    down, src = down.T, sources.T
    rev = reverse.reshape(-1, 128)
    theirs, pre, amat, ups, slopes = front(src, counts, x, down, up, ang)
    res, gmsg, got, gown = layer(x, cot, ups, slopes, theirs, rev, up, inner[0], outer[0])
    total = back(src, counts.reshape(1, -1), rev, got, gown, amat)
    grad_x, out = last(gmsg, total, pre, down, res)
    return out, grad_x


def solution(mesh):
    rows = P(("cluster", "narrow"))
    specs = (rows, rows, P(), P(), P(), P(), rows, rows, rows, rows)
    return jax.shard_map(
        on_device, mesh=mesh, in_specs=specs, out_specs=(rows, rows), check_vma=False
    )
```

```python
import functools
import jax
import jax.numpy as jnp
from jax import lax
from jax.experimental import pallas as pl
from jax.experimental.pallas import tpu as pltpu
from jax.sharding import PartitionSpec as P

CH = 4


def place():
    me = lax.axis_index("narrow")
    core = lax.rem(me, 2)
    far = lax.rem(lax.div(me, 2), 2)
    row = lax.div(me, 4)
    return row, far, core


def slot_of(row, far, core):
    return (lax.rem(row + 4, 4) * 2 + far) * 2 + core


ROOT_HALF = 0.7071067811865476
LAYER_TILES = 4
LAST_TILES = 4


def sigmoid(v):
    return 0.5 + 0.5 * jnp.tanh(0.5 * v)


def silu_both(v):
    s = sigmoid(v)
    f = v * s
    return f, s + f * (1.0 - s)


def low_lanes(shape):
    return lax.broadcasted_iota(jnp.int32, shape, len(shape) - 1) < 64


def swap_halves(v):
    return pltpu.roll(v, 64, 1)


def dot(a, b):
    return jnp.dot(a, b, preferred_element_type=jnp.float32)


def dot_rows(a, b):
    return lax.dot_general(a, b, (((1,), (1,)), ((), ())), preferred_element_type=jnp.float32)


def dot_cols(a, b):
    return lax.dot_general(a, b, (((0,), (0,)), ((), ())), preferred_element_type=jnp.float32)


def paired(v):
    n = v.shape[0] // 64
    v = v.reshape(n, 2, 32, 128)
    return jnp.where(low_lanes((n, 32, 128)), v[:, 0], v[:, 1]).reshape(n * 32, 128)


def spread(t):
    n = t.shape[0] // 32
    t = t.reshape(n, 32, 128)
    low = low_lanes(t.shape)
    zero = jnp.zeros_like(t)
    both = jnp.concatenate([jnp.where(low, t, zero), jnp.where(low, zero, t)], axis=1)
    return both.reshape(n * 64, 128)


def pick_rows(rev, table):
    edge = lax.rem(rev, 2048)
    block, rest = lax.div(edge, 64), lax.rem(edge, 64)
    row = block * 32 + lax.rem(rest, 32)
    upper = rest >= 32
    part = table.shape[0] // 4
    inner, outer = lax.rem(row, part), lax.div(row, part)
    hot = lax.broadcasted_iota(jnp.int32, (rev.shape[0], part), 1) == inner
    hot = jnp.where(hot, 1.0, 0.0).astype(jnp.bfloat16)
    wide = jnp.concatenate([table[j * part : (j + 1) * part] for j in range(4)], axis=1)
    four = dot(hot, wide)
    got = four[:, :128]
    for j in range(1, 4):
        got = jnp.where(outer == j, four[:, j * 128 : j * 128 + 128], got)
    return jnp.where(low_lanes(got.shape) != upper, got, 0.0)


EDGE_CHUNK = 512


def mirror_id():
    size = lax.axis_size("cluster")
    return {"cluster": lax.rem(lax.axis_index("cluster") + size // 2, size)}


def narrow_id(slot):
    return {"narrow": slot}


def send(src, dst, send_sem, recv_sem, target):
    return pltpu.make_async_remote_copy(
        src_ref=src,
        dst_ref=dst,
        send_sem=send_sem,
        recv_sem=recv_sem,
        device_id=target,
        device_id_type=pl.DeviceIdType.MESH,
    )


def hello(targets):
    barrier = pltpu.get_barrier_semaphore()
    for t in targets:
        pl.semaphore_signal(barrier, inc=1, device_id=t, device_id_type=pl.DeviceIdType.MESH)
    return lambda: pl.semaphore_wait(barrier, len(targets))


def relayout(ang, amat, tmp, k):
    low = low_lanes((64, 128))
    a = ang[k].astype(jnp.float32)
    for r in range(32):
        t = a[:, 128 * r : 128 * r + 128]
        tmp[16 * r : 16 * r + 8] = t
        tmp[16 * r + 8 : 16 * r + 16] = swap_halves(t)
    for s in range(0, 8, 2):
        first = tmp[pl.ds(s, 64, stride=8), :]
        second = tmp[pl.ds(s + 1, 64, stride=8), :]
        both = jnp.where(low, first, swap_halves(second)).astype(jnp.bfloat16)
        amat[pl.ds(pl.multiple_of(k * 64, 64), 64), s * 64 : s * 64 + 128] = both


def front_kernel(
    src, cnt, x, down, up_w, ang,
    theirs, pre_out, amat_out, up_out, slope_out,
    xbuf, abuf, trips, amat, pre, mine, rhs, tmp, ups, slopes,
    xsem, asem, osem, usem, ysend, yrecv, y2send, y2recv, zsend, zrecv, csend, crecv, msend, mrecv,
):
    row, far, core = place()
    up, dn = slot_of(row + 1, far, core), slot_of(row - 1, far, core)
    anti, sib = slot_of(row, 1 - far, core), slot_of(row, far, 1 - core)
    me = slot_of(row, far, core)
    nbr = (narrow_id(up), narrow_id(dn))
    anti_id, sib_id, mirror = narrow_id(anti), narrow_id(sib), mirror_id()
    group = trips.shape[0] // 16 // CH
    rows = group * 32
    half = {0: (0, 1), 1: (2, 3)}
    wd2 = jnp.concatenate([down[...]] * 2, axis=0)
    loads = []
    for q in range(CH):
        sl = pl.ds(q * 2 * rows, 2 * rows)
        loads.append(pltpu.make_async_copy(x.at[sl], xbuf.at[sl], xsem.at[q]))
        loads[-1].start()
    aload = pltpu.make_async_copy(ang, abuf, asem)
    aload.start()
    arrive = hello((*nbr, anti_id, sib_id, mirror))
    copies = []

    def go(c):
        c.start()
        copies.append(c)
        return c

    def part(slot, q):
        return trips.at[pl.ds((slot * CH + q) * group, group)]

    yc, y2, zc, cc = {}, {}, {}, []
    for q in range(CH):
        loads[q].wait()
        pair = paired(dot_rows(xbuf[q * 2 * rows : (q + 1) * 2 * rows], wd2))
        pre[q * rows : (q + 1) * rows] = pair
        fresh = (pair * sigmoid(pair)).astype(jnp.bfloat16)
        part(me, q)[...] = fresh.reshape(group, 32, 128)
        if q == 0:
            arrive()
        zc[q] = go(send(part(me, q), part(me, q), zsend.at[q], zrecv.at[q], anti_id))
        for d in (0, 1):
            yc[0, d, q] = go(
                send(part(me, q), part(me, q), ysend.at[0, d, q], yrecv.at[0, d, q], nbr[d])
            )
        cc.append(go(send(part(me, q), part(me, q), csend.at[0, q], crecv.at[0, q], sib_id)))
    outs = [pltpu.make_async_copy(pre, pre_out, osem.at[0])]
    outs[0].start()
    aload.wait()
    step = [0]
    blocks_n = amat.shape[0] // 64

    def lay(n):
        lo, hi = step[0], min(step[0] + n, blocks_n)
        step[0] = hi

        def one(k, carry):
            relayout(abuf, amat, tmp, k)
            return carry

        if hi > lo:
            lax.fori_loop(lo, hi, one, 0)

    def came(z, d):
        return slot_of(row - 1 if d == 0 else row + 1, far if z == 0 else 1 - far, core)

    def to_sib(slot, i, q):
        cc.append(go(send(part(slot, q), part(slot, q), csend.at[i, q], crecv.at[i, q], sib_id)))

    def pass_on(z, q):
        for d in (0, 1):
            yc[z, d, q].wait_recv()
            slot = came(z, d)
            if q in half[d]:
                y2[z, q] = go(send(part(slot, q), part(slot, q), y2send.at[z, q], y2recv.at[z, q], nbr[d]))
            to_sib(slot, 1 + z * 4 + d, q)

    def from_far(q):
        zc[q].wait_recv()
        for d in (0, 1):
            yc[1, d, q] = go(
                send(part(anti, q), part(anti, q), ysend.at[1, d, q], yrecv.at[1, d, q], nbr[d])
            )
        to_sib(anti, 3, q)

    def far_row(z, q):
        y2[z, q].wait_recv()
        to_sib(slot_of(row + 2, far if z == 0 else 1 - far, core), 4 if z == 0 else 7, q)

    lay(6)
    pass_on(0, 0)
    lay(4)
    pass_on(0, 1)
    lay(4)
    pass_on(0, 2)
    from_far(0)
    lay(3)
    pass_on(0, 3)
    lay(3)
    from_far(1)
    lay(4)
    far_row(0, 0)
    far_row(0, 2)
    from_far(2)
    lay(4)
    pass_on(1, 0)
    far_row(0, 1)
    far_row(0, 3)
    from_far(3)
    lay(blocks_n)
    outs.append(pltpu.make_async_copy(amat, amat_out, osem.at[1]))
    outs[1].start()
    for q in range(1, CH):
        pass_on(1, q)
    for q in range(CH):
        far_row(1, q)
    for c in cc:
        c.wait_recv()

    per = blocks_n // CH
    mc = []
    for q in range(CH):

        def one(p, carry, q=q):
            for e in (0, 1):
                k = p * 2 + e
                used = jnp.broadcast_to(cnt[k], (32, 128))
                for s in range(8):
                    v = trips[lax.rem(src[s, k], trips.shape[0])]
                    v = jnp.where(used > s, v, jnp.zeros_like(v))
                    rhs[e, s * 64 : s * 64 + 32] = v
                    rhs[e, s * 64 + 32 : s * 64 + 64] = swap_halves(v)
            for e in (0, 1):
                k = p * 2 + e
                o = dot(amat[pl.ds(pl.multiple_of(k * 64, 64), 64), :], rhs[e])
                pair = jnp.where(low_lanes((32, 128)), o[:32], swap_halves(o[32:]))
                mine[pl.ds(pl.multiple_of(k * 32, 32), 32), :] = pair.astype(jnp.bfloat16)
            return carry

        lax.fori_loop(q * per // 2, (q + 1) * per // 2, one, 0)
        sl = pl.ds(q * rows, rows)
        mc.append(go(send(mine.at[sl], theirs.at[sl], msend.at[q], mrecv.at[q], mirror)))
    w2 = jnp.concatenate([up_w[...]] * 2, axis=0)
    for q in range(CH):

        def raise_tile(i, carry):
            own = mine[pl.ds(pl.multiple_of(i * 128, 128), 128), :]
            value, slope = silu_both(dot(spread(own), w2))
            sl = pl.ds(pl.multiple_of(i * 256, 256), 256)
            ups[sl, :] = value.astype(jnp.bfloat16)
            slopes[sl, :] = slope.astype(jnp.bfloat16)
            return carry

        lax.fori_loop(q * rows // 128, (q + 1) * rows // 128, raise_tile, 0)
        sl = pl.ds(q * 2 * rows, 2 * rows)
        for j, (a, b) in enumerate(((ups, up_out), (slopes, slope_out))):
            outs.append(pltpu.make_async_copy(a.at[sl], b.at[sl], usem.at[j, q]))
            outs[-1].start()
    for c in mc:
        c.wait_recv()
    for c in copies:
        c.wait_send()
    for c in outs:
        c.wait()


def front(src, cnt, x, down, up, ang):
    n = x.shape[0]
    dma = pltpu.SemaphoreType.DMA
    vm = pltpu.VMEM
    bf, f32 = jnp.bfloat16, jnp.float32
    anywhere = pl.BlockSpec(memory_space=pl.ANY)
    smem = pl.BlockSpec(memory_space=pltpu.SMEM)
    return pl.pallas_call(
        front_kernel,
        name="front",
        in_specs=[smem, smem, anywhere] + [pl.BlockSpec(memory_space=vm)] * 2 + [anywhere],
        out_specs=[anywhere] * 5,
        out_shape=[
            jax.ShapeDtypeStruct((n // 2, 128), bf),
            jax.ShapeDtypeStruct((n // 2, 128), f32),
            jax.ShapeDtypeStruct((n, 512), bf),
            jax.ShapeDtypeStruct((n, 512), bf),
            jax.ShapeDtypeStruct((n, 512), bf),
        ],
        scratch_shapes=[
            vm(x.shape, bf),
            vm(ang.shape, bf),
            vm((n // 4, 32, 128), bf),
            vm((n, 512), bf),
            vm((n // 2, 128), f32),
            vm((n // 2, 128), bf),
            vm((2, 512, 128), bf),
            vm((512, 128), f32),
            vm((n, 512), bf),
            vm((n, 512), bf),
            dma((CH,)),
            dma,
            dma((2,)),
            dma((2, CH)),
            dma((2, 2, CH)),
            dma((2, 2, CH)),
            dma((2, CH)),
            dma((2, CH)),
            dma((CH,)),
            dma((CH,)),
            dma((8, CH)),
            dma((8, CH)),
            dma((CH,)),
            dma((CH,)),
        ],
        compiler_params=pltpu.CompilerParams(collective_id=0, has_side_effects=True),
    )(src, cnt, x, down, up, ang)


def layer_kernel(x, cot, ups, slopes, theirs, rev, up_w, wi, wo, out, gmsg, got, gown, hs, col, ssem, rsem):
    i = pl.program_id(0)
    mirror = mirror_id()

    @pl.when(i == 0)
    def _():
        hello((mirror,))()
        columns(rev, col)

    c = ROOT_HALF
    w2 = jnp.concatenate([up_w[...]] * 2, axis=0)
    here = pl.ds(pl.multiple_of(i * x.shape[0], x.shape[0]), x.shape[0])
    up, dup = ups[...].astype(jnp.float32), slopes[...].astype(jnp.float32)
    picked = pick_rows(col[here, :], theirs[...]).astype(jnp.bfloat16)
    pup, dpup = silu_both(dot(picked, w2))
    pup = pup.astype(jnp.bfloat16).astype(jnp.float32)
    hidden = (x[...].astype(jnp.float32) + (up + pup) * c) * c
    act, dact = silu_both(dot(hidden.astype(jnp.bfloat16), wi[...]))
    res, dres = silu_both(dot(act.astype(jnp.bfloat16), wo[...]))
    out[...] = ((hidden + res) * c).astype(jnp.bfloat16)
    scaled = cot[...].astype(jnp.float32) * c
    grad_out = (scaled * dres).astype(jnp.bfloat16)
    grad_in = (dot_rows(grad_out, wo[...]) * dact).astype(jnp.bfloat16)
    grad_msg = (scaled + dot_rows(grad_in, wi[...])) * c
    gmsg[...] = grad_msg.astype(jnp.bfloat16)
    rounded = grad_msg.astype(jnp.bfloat16).astype(jnp.float32)
    part = (rounded * (c * dpup)).astype(jnp.bfloat16)
    tile = hs.shape[0] // LAYER_TILES

    def piece(n):
        sl = pl.ds(pl.multiple_of(n * tile, tile), tile)
        return send(hs.at[sl], got.at[sl], ssem.at[n], rsem.at[n], mirror)

    hs[pl.ds(pl.multiple_of(i * tile, tile), tile), :] = paired(dot_rows(part, w2)).astype(jnp.bfloat16)
    piece(i).start()
    gown[...] = dot_rows((grad_msg * (c * dup)).astype(jnp.bfloat16), w2)

    @pl.when(i == LAYER_TILES - 1)
    def _():
        for n in range(LAYER_TILES):
            piece(n).wait()


def layer(x, cot, ups, slopes, theirs, rev, up, wi, wo):
    n, d = x.shape
    t = n // LAYER_TILES
    wide = pl.BlockSpec((t, d), lambda i: (i, 0))

    def whole(a):
        return pl.BlockSpec(a.shape, lambda i: (0, 0))

    return pl.pallas_call(
        layer_kernel,
        name="layer",
        grid=(LAYER_TILES,),
        in_specs=[
            wide,
            wide,
            wide,
            wide,
            whole(theirs),
            whole(rev),
            whole(up),
            whole(wi),
            whole(wo),
        ],
        out_specs=[
            wide,
            wide,
            pl.BlockSpec(memory_space=pl.ANY),
            pl.BlockSpec((t, 128), lambda i: (i, 0)),
        ],
        out_shape=[
            jax.ShapeDtypeStruct((n, d), jnp.bfloat16),
            jax.ShapeDtypeStruct((n, d), jnp.bfloat16),
            jax.ShapeDtypeStruct((n // 2, 128), jnp.bfloat16),
            jax.ShapeDtypeStruct((n, 128), jnp.float32),
        ],
        scratch_shapes=[
            pltpu.VMEM((n // 2, 128), jnp.bfloat16),
            pltpu.VMEM((n, 1), jnp.int32),
            pltpu.SemaphoreType.DMA((LAYER_TILES,)),
            pltpu.SemaphoreType.DMA((LAYER_TILES,)),
        ],
        compiler_params=pltpu.CompilerParams(collective_id=2, has_side_effects=True),
    )(x, cot, ups, slopes, theirs, rev, up, wi, wo)


def columns(rev, col):
    turned = jnp.transpose(rev[...])
    for j in range(rev.shape[0]):
        col[j * 128 : (j + 1) * 128, :] = turned[:, j : j + 1]


def slot_row(src, cnt):
    slots, n = src.shape
    named = lax.rem(src[...], 512)
    used = lax.broadcasted_iota(jnp.int32, (slots, n), 0) < cnt[...]
    named = jnp.where(used, named, -1).astype(jnp.float32)
    wide = jnp.concatenate([named] * 4, axis=1)
    shape = (slots, 4 * n)
    group = lax.div(lax.broadcasted_iota(jnp.int32, shape, 1), n)
    own = lax.rem(lax.broadcasted_iota(jnp.int32, shape, 0), 4)
    kept = jnp.where(group == own, wide, 0.0)
    halves = [jnp.sum(kept[4 * h : 4 * h + 4], axis=0, keepdims=True) for h in (0, 1)]
    return jnp.concatenate(halves, axis=1)


def back_kernel(
    src, cnt, rev, got, gown_in, amat_in,
    out,
    gown, amat, lsem, col, pairs, hot, parts, near_buf, y2buf, ybuf, zbuf, stage, acc,
    psend, precv, y2send, y2recv, ysend, yrecv, zsend, zrecv,
):
    row, far, core = place()
    up, dn = slot_of(row + 1, far, core), slot_of(row - 1, far, core)
    anti, sib = slot_of(row, 1 - far, core), slot_of(row, far, 1 - core)
    nbr = (narrow_id(up), narrow_id(dn))
    anti_id, sib_id = narrow_id(anti), narrow_id(sib)
    half = {0: (0, 1), 1: (2, 3)}
    arrive = hello((*nbr, anti_id, sib_id))
    loads = [
        pltpu.make_async_copy(gown_in, gown, lsem.at[0]),
        pltpu.make_async_copy(amat_in, amat, lsem.at[1]),
    ]
    for c in loads:
        c.start()
    columns(rev, col)

    shape = (512, 256)
    at = lax.broadcasted_iota(jnp.int32, shape, 0)
    named = ((lax.rem(lax.div(at, 32), 4) * 2 + lax.rem(lax.div(at, 128), 2)) * 2 + lax.div(at, 256)) * 32
    named = (named + lax.rem(at, 32)).astype(jnp.float32)
    hot[...] = jnp.where(named == slot_row(src, cnt), 1.0, 0.0).astype(jnp.bfloat16)
    tile = 512

    def tiles(i, carry):
        sl = pl.ds(pl.multiple_of(i * tile, tile), tile)
        theirs = pick_rows(col[sl, :], got[...])
        grad = (gown[sl, :] + theirs + swap_halves(theirs)).astype(jnp.bfloat16)
        for k in range(tile // 64):
            a = amat[pl.ds(pl.multiple_of(i * tile + k * 64, 64), 64), :]
            pair = paired(dot_cols(a, grad[k * 64 : k * 64 + 64]))
            for s in range(8):
                to = pl.multiple_of((s * 32 + i * (tile // 64) + k) * 32, 32)
                pairs[pl.ds(to, 32), :] = pair[s * 32 : s * 32 + 32]
        return carry

    for c in loads:
        c.wait()
    lax.fori_loop(0, gown.shape[0] // tile, tiles, 0)
    copies = []

    def go(c):
        c.start()
        copies.append(c)
        return c

    sc, y2, yc, zc = {}, {}, {}, {}
    far_of = (1 - far, far)
    bf = jnp.bfloat16

    def build(q):
        def one(g, carry):
            t = [pairs[pl.ds(g * 2 + e, 256, stride=32), :].astype(bf) for e in (0, 1)]
            both = dot(hot[...], jnp.concatenate(t, axis=1)).astype(bf)
            for e in (0, 1):
                parts[g * 2 + e] = both[:, e * 128 : e * 128 + 128]
            return carry

        lax.fori_loop(4 * q, 4 * q + 4, one, 0)
        sl = pl.ds(8 * q, 8)
        mate = pl.ds(pl.multiple_of((1 - core) * 256, 256), 256)
        sc[q] = go(send(parts.at[sl, mate], near_buf.at[sl], psend.at[q], precv.at[q], sib_id))

    def chip_sum(z, o, q):
        sl = pl.ds(8 * q, 8)
        to = far_of[z] * 128 + lax.rem(row + o, 4) * 32
        a = parts[sl, pl.ds(pl.multiple_of(core * 256 + to, 32), 32), :]
        b = near_buf[sl, pl.ds(pl.multiple_of(to, 32), 32), :]
        return a.astype(jnp.float32) + b.astype(jnp.float32)

    def first(z, q):
        sl = pl.ds(8 * q, 8)
        d = 0 if q in half[0] else 1
        stage[z, 2, sl] = chip_sum(z, 2, q).astype(bf)
        y2[z, q] = go(send(stage.at[z, 2, sl], y2buf.at[z, sl], y2send.at[z, q], y2recv.at[z, q], nbr[d]))
        e = 1 - d
        o = 1 if e == 0 else 3
        stage[z, o, sl] = chip_sum(z, o, q).astype(bf)
        yc[z, e, q] = go(send(stage.at[z, o, sl], ybuf.at[z, e, sl], ysend.at[z, e, q], yrecv.at[z, e, q], nbr[e]))

    def second(z, q):
        sl = pl.ds(8 * q, 8)
        d = 0 if q in half[0] else 1
        o = 1 if d == 0 else 3
        y2[z, q].wait_recv()
        stage[z, o, sl] = (chip_sum(z, o, q) + y2buf[z, sl].astype(jnp.float32)).astype(bf)
        yc[z, d, q] = go(send(stage.at[z, o, sl], ybuf.at[z, d, sl], ysend.at[z, d, q], yrecv.at[z, d, q], nbr[d]))

    def final(z, q):
        sl = pl.ds(8 * q, 8)
        yc[z, 0, q].wait_recv()
        yc[z, 1, q].wait_recv()
        return (
            chip_sum(z, 0, q)
            + ybuf[z, 0, sl].astype(jnp.float32)
            + ybuf[z, 1, sl].astype(jnp.float32)
        )

    order = (0, 2, 1, 3)
    arrive()
    build(order[0])
    for i in range(CH):
        if i + 1 < CH:
            build(order[i + 1])
        sc[order[i]].wait_recv()
        first(0, order[i])
    for q in order:
        second(0, q)
        first(1, q)
    for q in order:
        sl = pl.ds(8 * q, 8)
        stage[0, 0, sl] = final(0, q).astype(bf)
        zc[q] = go(send(stage.at[0, 0, sl], zbuf.at[sl], zsend.at[q], zrecv.at[q], anti_id))
        second(1, q)
    for q in order:
        acc[pl.ds(8 * q, 8)] = final(1, q)
    for q in order:
        sl = pl.ds(8 * q, 8)
        zc[q].wait_recv()
        total = acc[sl] + zbuf[sl].astype(jnp.float32)
        for r in range(8):
            out[pl.ds(8 * q + r, 32, stride=32), :] = total[r]
    for c in copies:
        c.wait_send()


def back(src, cnt, rev, got, gown, amat):
    dma = pltpu.SemaphoreType.DMA
    vm = pltpu.VMEM
    bf, f32 = jnp.bfloat16, jnp.float32
    inside = pl.BlockSpec(memory_space=vm)
    return pl.pallas_call(
        back_kernel,
        name="back",
        in_specs=[inside] * 4 + [pl.BlockSpec(memory_space=pl.ANY)] * 2,
        out_specs=inside,
        out_shape=jax.ShapeDtypeStruct((1024, 128), f32),
        scratch_shapes=[
            vm(gown.shape, f32),
            vm(amat.shape, bf),
            dma((2,)),
            vm((2048, 1), jnp.int32),
            vm((8192, 128), f32),
            vm((512, 256), bf),
            vm((32, 512, 128), bf),
            vm((32, 256, 128), bf),
            vm((2, 32, 32, 128), bf),
            vm((2, 2, 32, 32, 128), bf),
            vm((32, 32, 128), bf),
            vm((2, 4, 32, 32, 128), bf),
            vm((32, 32, 128), f32),
            dma((CH,)),
            dma((CH,)),
            dma((2, CH)),
            dma((2, CH)),
            dma((2, 2, CH)),
            dma((2, 2, CH)),
            dma((CH,)),
            dma((CH,)),
        ],
        compiler_params=pltpu.CompilerParams(collective_id=1, has_side_effects=True),
    )(src, cnt, rev, got, gown, amat)


def last_kernel(gmsg, total, pre, down, res, out, res_out):
    res_out[...] = res[...]
    grad = (total[...] * silu_both(pre[...])[1]).astype(jnp.bfloat16)
    w = jnp.concatenate([down[...]] * 2, axis=0)
    out[...] = (gmsg[...].astype(jnp.float32) + dot(spread(grad), w)).astype(jnp.bfloat16)


def last(gmsg, total, pre, down, res):
    n, d = gmsg.shape
    t = n // LAST_TILES
    wide = pl.BlockSpec((t, d), lambda i: (i, 0))
    slim = pl.BlockSpec((t // 2, 128), lambda i: (i, 0))
    return pl.pallas_call(
        last_kernel,
        name="last",
        grid=(LAST_TILES,),
        in_specs=[wide, slim, slim, pl.BlockSpec(down.shape, lambda i: (0, 0)), wide],
        out_specs=[wide, wide],
        out_shape=[jax.ShapeDtypeStruct((n, d), jnp.bfloat16)] * 2,
    )(gmsg, total, pre, down, res)


def on_device(x, cot, down, up, inner, outer, ang, reverse, sources, counts):
    down, src = down.T, sources.T
    rev = reverse.reshape(-1, 128)
    theirs, pre, amat, ups, slopes = front(src, counts, x, down, up, ang)
    res, gmsg, got, gown = layer(x, cot, ups, slopes, theirs, rev, up, inner[0], outer[0])
    total = back(src, counts.reshape(1, -1), rev, got, gown, amat)
    grad_x, out = last(gmsg, total, pre, down, res)
    return out, grad_x


def solution(mesh):
    rows = P(("cluster", "narrow"))
    specs = (rows, rows, P(), P(), P(), P(), rows, rows, rows, rows)
    return jax.shard_map(
        on_device, mesh=mesh, in_specs=specs, out_specs=(rows, rows), check_vma=False
    )
```

```python
import functools
import jax
import jax.numpy as jnp
from jax import lax
from jax.experimental import pallas as pl
from jax.experimental.pallas import tpu as pltpu
from jax.sharding import PartitionSpec as P

CH = 4
MIRROR_PARTS = 8


def place():
    me = lax.axis_index("narrow")
    core = lax.rem(me, 2)
    far = lax.rem(lax.div(me, 2), 2)
    row = lax.div(me, 4)
    return row, far, core


def slot_of(row, far, core):
    return (lax.rem(row + 4, 4) * 2 + far) * 2 + core


ROOT_HALF = 0.7071067811865476
LAYER_TILES = 4
LAST_TILES = 4


def sigmoid(v):
    return 0.5 + 0.5 * jnp.tanh(0.5 * v)


def silu_both(v):
    s = sigmoid(v)
    f = v * s
    return f, s + f * (1.0 - s)


def low_lanes(shape):
    return lax.broadcasted_iota(jnp.int32, shape, len(shape) - 1) < 64


def swap_halves(v):
    return pltpu.roll(v, 64, 1)


def dot(a, b):
    return jnp.dot(a, b, preferred_element_type=jnp.float32)


def dot_rows(a, b):
    return lax.dot_general(a, b, (((1,), (1,)), ((), ())), preferred_element_type=jnp.float32)


def dot_cols(a, b):
    return lax.dot_general(a, b, (((0,), (0,)), ((), ())), preferred_element_type=jnp.float32)


def paired(v):
    n = v.shape[0] // 64
    v = v.reshape(n, 2, 32, 128)
    return jnp.where(low_lanes((n, 32, 128)), v[:, 0], v[:, 1]).reshape(n * 32, 128)


def spread(t):
    n = t.shape[0] // 32
    t = t.reshape(n, 32, 128)
    low = low_lanes(t.shape)
    zero = jnp.zeros_like(t)
    both = jnp.concatenate([jnp.where(low, t, zero), jnp.where(low, zero, t)], axis=1)
    return both.reshape(n * 64, 128)


def pick_rows(rev, table):
    edge = lax.rem(rev, 2048)
    block, rest = lax.div(edge, 64), lax.rem(edge, 64)
    row = block * 32 + lax.rem(rest, 32)
    upper = rest >= 32
    part = table.shape[0] // 4
    inner, outer = lax.rem(row, part), lax.div(row, part)
    hot = lax.broadcasted_iota(jnp.int32, (rev.shape[0], part), 1) == inner
    hot = jnp.where(hot, 1.0, 0.0).astype(jnp.bfloat16)
    wide = jnp.concatenate([table[j * part : (j + 1) * part] for j in range(4)], axis=1)
    four = dot(hot, wide)
    got = four[:, :128]
    for j in range(1, 4):
        got = jnp.where(outer == j, four[:, j * 128 : j * 128 + 128], got)
    return jnp.where(low_lanes(got.shape) != upper, got, 0.0)


EDGE_CHUNK = 512


def mirror_id():
    size = lax.axis_size("cluster")
    return {"cluster": lax.rem(lax.axis_index("cluster") + size // 2, size)}


def narrow_id(slot):
    return {"narrow": slot}


def send(src, dst, send_sem, recv_sem, target):
    return pltpu.make_async_remote_copy(
        src_ref=src,
        dst_ref=dst,
        send_sem=send_sem,
        recv_sem=recv_sem,
        device_id=target,
        device_id_type=pl.DeviceIdType.MESH,
    )


def hello(targets):
    barrier = pltpu.get_barrier_semaphore()
    for t in targets:
        pl.semaphore_signal(barrier, inc=1, device_id=t, device_id_type=pl.DeviceIdType.MESH)
    return lambda: pl.semaphore_wait(barrier, len(targets))


def relayout(ang, amat, tmp, k):
    low = low_lanes((64, 128))
    a = ang[k].astype(jnp.float32)
    for r in range(32):
        t = a[:, 128 * r : 128 * r + 128]
        tmp[16 * r : 16 * r + 8] = t
        tmp[16 * r + 8 : 16 * r + 16] = swap_halves(t)
    for s in range(0, 8, 2):
        first = tmp[pl.ds(s, 64, stride=8), :]
        second = tmp[pl.ds(s + 1, 64, stride=8), :]
        both = jnp.where(low, first, swap_halves(second)).astype(jnp.bfloat16)
        amat[pl.ds(pl.multiple_of(k * 64, 64), 64), s * 64 : s * 64 + 128] = both


def front_kernel(
    src, cnt, x, down, up_w, ang,
    theirs, pre_out, amat_out, up_out, slope_out,
    xbuf, abuf, trips, amat, pre, mine, rhs, tmp, ups, slopes,
    xsem, asem, osem, usem, ysend, yrecv, y2send, y2recv, zsend, zrecv, csend, crecv, msend, mrecv,
):
    row, far, core = place()
    up, dn = slot_of(row + 1, far, core), slot_of(row - 1, far, core)
    anti, sib = slot_of(row, 1 - far, core), slot_of(row, far, 1 - core)
    me = slot_of(row, far, core)
    nbr = (narrow_id(up), narrow_id(dn))
    anti_id, sib_id, mirror = narrow_id(anti), narrow_id(sib), mirror_id()
    group = trips.shape[0] // 16 // CH
    rows = group * 32
    half = {0: (0, 1), 1: (2, 3)}
    wd2 = jnp.concatenate([down[...]] * 2, axis=0)
    loads = []
    for q in range(CH):
        sl = pl.ds(q * 2 * rows, 2 * rows)
        loads.append(pltpu.make_async_copy(x.at[sl], xbuf.at[sl], xsem.at[q]))
        loads[-1].start()
    aload = pltpu.make_async_copy(ang, abuf, asem)
    aload.start()
    arrive = hello((*nbr, anti_id, sib_id, mirror))
    copies = []

    def go(c):
        c.start()
        copies.append(c)
        return c

    def part(slot, q):
        return trips.at[pl.ds((slot * CH + q) * group, group)]

    yc, y2, zc, cc = {}, {}, {}, []
    for q in range(CH):
        loads[q].wait()
        pair = paired(dot_rows(xbuf[q * 2 * rows : (q + 1) * 2 * rows], wd2))
        pre[q * rows : (q + 1) * rows] = pair
        fresh = (pair * sigmoid(pair)).astype(jnp.bfloat16)
        part(me, q)[...] = fresh.reshape(group, 32, 128)
        if q == 0:
            arrive()
        zc[q] = go(send(part(me, q), part(me, q), zsend.at[q], zrecv.at[q], anti_id))
        for d in (0, 1):
            yc[0, d, q] = go(
                send(part(me, q), part(me, q), ysend.at[0, d, q], yrecv.at[0, d, q], nbr[d])
            )
        cc.append(go(send(part(me, q), part(me, q), csend.at[0, q], crecv.at[0, q], sib_id)))
    outs = [pltpu.make_async_copy(pre, pre_out, osem.at[0])]
    outs[0].start()
    aload.wait()
    step = [0]
    blocks_n = amat.shape[0] // 64

    def lay(n):
        lo, hi = step[0], min(step[0] + n, blocks_n)
        step[0] = hi

        def one(k, carry):
            relayout(abuf, amat, tmp, k)
            return carry

        if hi > lo:
            lax.fori_loop(lo, hi, one, 0)

    def came(z, d):
        return slot_of(row - 1 if d == 0 else row + 1, far if z == 0 else 1 - far, core)

    def to_sib(slot, i, q):
        cc.append(go(send(part(slot, q), part(slot, q), csend.at[i, q], crecv.at[i, q], sib_id)))

    def pass_on(z, q):
        for d in (0, 1):
            yc[z, d, q].wait_recv()
            slot = came(z, d)
            if q in half[d]:
                y2[z, q] = go(send(part(slot, q), part(slot, q), y2send.at[z, q], y2recv.at[z, q], nbr[d]))
            to_sib(slot, 1 + z * 4 + d, q)

    def from_far(q):
        zc[q].wait_recv()
        for d in (0, 1):
            yc[1, d, q] = go(
                send(part(anti, q), part(anti, q), ysend.at[1, d, q], yrecv.at[1, d, q], nbr[d])
            )
        to_sib(anti, 3, q)

    def far_row(z, q):
        y2[z, q].wait_recv()
        to_sib(slot_of(row + 2, far if z == 0 else 1 - far, core), 4 if z == 0 else 7, q)

    lay(6)
    pass_on(0, 0)
    lay(4)
    pass_on(0, 1)
    lay(4)
    pass_on(0, 2)
    from_far(0)
    lay(3)
    pass_on(0, 3)
    lay(3)
    from_far(1)
    lay(4)
    far_row(0, 0)
    far_row(0, 2)
    from_far(2)
    lay(4)
    pass_on(1, 0)
    far_row(0, 1)
    far_row(0, 3)
    from_far(3)
    lay(blocks_n)
    outs.append(pltpu.make_async_copy(amat, amat_out, osem.at[1]))
    outs[1].start()
    for q in range(1, CH):
        pass_on(1, q)
    for q in range(CH):
        far_row(1, q)
    for c in cc:
        c.wait_recv()

    per = blocks_n // MIRROR_PARTS
    span = mine.shape[0] // MIRROR_PARTS
    mc = []
    for q in range(MIRROR_PARTS):

        def one(p, carry, q=q):
            for e in (0, 1):
                k = p * 2 + e
                used = jnp.broadcast_to(cnt[k], (32, 128))
                for s in range(8):
                    v = trips[lax.rem(src[s, k], trips.shape[0])]
                    v = jnp.where(used > s, v, jnp.zeros_like(v))
                    rhs[e, s * 64 : s * 64 + 32] = v
                    rhs[e, s * 64 + 32 : s * 64 + 64] = swap_halves(v)
            for e in (0, 1):
                k = p * 2 + e
                o = dot(amat[pl.ds(pl.multiple_of(k * 64, 64), 64), :], rhs[e])
                pair = jnp.where(low_lanes((32, 128)), o[:32], swap_halves(o[32:]))
                mine[pl.ds(pl.multiple_of(k * 32, 32), 32), :] = pair.astype(jnp.bfloat16)
            return carry

        lax.fori_loop(q * per // 2, (q + 1) * per // 2, one, 0)
        sl = pl.ds(q * span, span)
        mc.append(go(send(mine.at[sl], theirs.at[sl], msend.at[q], mrecv.at[q], mirror)))
    w2 = jnp.concatenate([up_w[...]] * 2, axis=0)
    for q in range(CH):

        def raise_tile(i, carry):
            own = mine[pl.ds(pl.multiple_of(i * 128, 128), 128), :]
            value, slope = silu_both(dot(spread(own), w2))
            sl = pl.ds(pl.multiple_of(i * 256, 256), 256)
            ups[sl, :] = value.astype(jnp.bfloat16)
            slopes[sl, :] = slope.astype(jnp.bfloat16)
            return carry

        lax.fori_loop(q * rows // 128, (q + 1) * rows // 128, raise_tile, 0)
        sl = pl.ds(q * 2 * rows, 2 * rows)
        for j, (a, b) in enumerate(((ups, up_out), (slopes, slope_out))):
            outs.append(pltpu.make_async_copy(a.at[sl], b.at[sl], usem.at[j, q]))
            outs[-1].start()
    for c in mc:
        c.wait_recv()
    for c in copies:
        c.wait_send()
    for c in outs:
        c.wait()


def front(src, cnt, x, down, up, ang):
    n = x.shape[0]
    dma = pltpu.SemaphoreType.DMA
    vm = pltpu.VMEM
    bf, f32 = jnp.bfloat16, jnp.float32
    anywhere = pl.BlockSpec(memory_space=pl.ANY)
    smem = pl.BlockSpec(memory_space=pltpu.SMEM)
    return pl.pallas_call(
        front_kernel,
        name="front",
        in_specs=[smem, smem, anywhere] + [pl.BlockSpec(memory_space=vm)] * 2 + [anywhere],
        out_specs=[anywhere] * 5,
        out_shape=[
            jax.ShapeDtypeStruct((n // 2, 128), bf),
            jax.ShapeDtypeStruct((n // 2, 128), f32),
            jax.ShapeDtypeStruct((n, 512), bf),
            jax.ShapeDtypeStruct((n, 512), bf),
            jax.ShapeDtypeStruct((n, 512), bf),
        ],
        scratch_shapes=[
            vm(x.shape, bf),
            vm(ang.shape, bf),
            vm((n // 4, 32, 128), bf),
            vm((n, 512), bf),
            vm((n // 2, 128), f32),
            vm((n // 2, 128), bf),
            vm((2, 512, 128), bf),
            vm((512, 128), f32),
            vm((n, 512), bf),
            vm((n, 512), bf),
            dma((CH,)),
            dma,
            dma((2,)),
            dma((2, CH)),
            dma((2, 2, CH)),
            dma((2, 2, CH)),
            dma((2, CH)),
            dma((2, CH)),
            dma((CH,)),
            dma((CH,)),
            dma((8, CH)),
            dma((8, CH)),
            dma((MIRROR_PARTS,)),
            dma((MIRROR_PARTS,)),
        ],
        compiler_params=pltpu.CompilerParams(collective_id=0, has_side_effects=True),
    )(src, cnt, x, down, up, ang)


def layer_kernel(x, cot, ups, slopes, theirs, rev, up_w, wi, wo, out, gmsg, got, gown, hs, col, ssem, rsem):
    i = pl.program_id(0)
    mirror = mirror_id()

    @pl.when(i == 0)
    def _():
        hello((mirror,))()
        columns(rev, col)

    c = ROOT_HALF
    w2 = jnp.concatenate([up_w[...]] * 2, axis=0)
    here = pl.ds(pl.multiple_of(i * x.shape[0], x.shape[0]), x.shape[0])
    up, dup = ups[...].astype(jnp.float32), slopes[...].astype(jnp.float32)
    picked = pick_rows(col[here, :], theirs[...]).astype(jnp.bfloat16)
    pup, dpup = silu_both(dot(picked, w2))
    pup = pup.astype(jnp.bfloat16).astype(jnp.float32)
    hidden = (x[...].astype(jnp.float32) + (up + pup) * c) * c
    act, dact = silu_both(dot(hidden.astype(jnp.bfloat16), wi[...]))
    res, dres = silu_both(dot(act.astype(jnp.bfloat16), wo[...]))
    out[...] = ((hidden + res) * c).astype(jnp.bfloat16)
    scaled = cot[...].astype(jnp.float32) * c
    grad_out = (scaled * dres).astype(jnp.bfloat16)
    grad_in = (dot_rows(grad_out, wo[...]) * dact).astype(jnp.bfloat16)
    grad_msg = (scaled + dot_rows(grad_in, wi[...])) * c
    gmsg[...] = grad_msg.astype(jnp.bfloat16)
    rounded = grad_msg.astype(jnp.bfloat16).astype(jnp.float32)
    part = (rounded * (c * dpup)).astype(jnp.bfloat16)
    tile = hs.shape[0] // LAYER_TILES

    def piece(n):
        sl = pl.ds(pl.multiple_of(n * tile, tile), tile)
        return send(hs.at[sl], got.at[sl], ssem.at[n], rsem.at[n], mirror)

    hs[pl.ds(pl.multiple_of(i * tile, tile), tile), :] = paired(dot_rows(part, w2)).astype(jnp.bfloat16)
    piece(i).start()
    gown[...] = dot_rows((grad_msg * (c * dup)).astype(jnp.bfloat16), w2)

    @pl.when(i == LAYER_TILES - 1)
    def _():
        for n in range(LAYER_TILES):
            piece(n).wait()


def layer(x, cot, ups, slopes, theirs, rev, up, wi, wo):
    n, d = x.shape
    t = n // LAYER_TILES
    wide = pl.BlockSpec((t, d), lambda i: (i, 0))

    def whole(a):
        return pl.BlockSpec(a.shape, lambda i: (0, 0))

    return pl.pallas_call(
        layer_kernel,
        name="layer",
        grid=(LAYER_TILES,),
        in_specs=[
            wide,
            wide,
            wide,
            wide,
            whole(theirs),
            whole(rev),
            whole(up),
            whole(wi),
            whole(wo),
        ],
        out_specs=[
            wide,
            wide,
            pl.BlockSpec(memory_space=pl.ANY),
            pl.BlockSpec((t, 128), lambda i: (i, 0)),
        ],
        out_shape=[
            jax.ShapeDtypeStruct((n, d), jnp.bfloat16),
            jax.ShapeDtypeStruct((n, d), jnp.bfloat16),
            jax.ShapeDtypeStruct((n // 2, 128), jnp.bfloat16),
            jax.ShapeDtypeStruct((n, 128), jnp.float32),
        ],
        scratch_shapes=[
            pltpu.VMEM((n // 2, 128), jnp.bfloat16),
            pltpu.VMEM((n, 1), jnp.int32),
            pltpu.SemaphoreType.DMA((LAYER_TILES,)),
            pltpu.SemaphoreType.DMA((LAYER_TILES,)),
        ],
        compiler_params=pltpu.CompilerParams(collective_id=2, has_side_effects=True),
    )(x, cot, ups, slopes, theirs, rev, up, wi, wo)


def columns(rev, col):
    turned = jnp.transpose(rev[...])
    for j in range(rev.shape[0]):
        col[j * 128 : (j + 1) * 128, :] = turned[:, j : j + 1]


def slot_row(src, cnt):
    slots, n = src.shape
    named = lax.rem(src[...], 512)
    used = lax.broadcasted_iota(jnp.int32, (slots, n), 0) < cnt[...]
    named = jnp.where(used, named, -1).astype(jnp.float32)
    wide = jnp.concatenate([named] * 4, axis=1)
    shape = (slots, 4 * n)
    group = lax.div(lax.broadcasted_iota(jnp.int32, shape, 1), n)
    own = lax.rem(lax.broadcasted_iota(jnp.int32, shape, 0), 4)
    kept = jnp.where(group == own, wide, 0.0)
    halves = [jnp.sum(kept[4 * h : 4 * h + 4], axis=0, keepdims=True) for h in (0, 1)]
    return jnp.concatenate(halves, axis=1)


def back_kernel(
    src, cnt, rev, got, gown_in, amat_in,
    out,
    gown, amat, lsem, col, pairs, hot, parts, near_buf, y2buf, ybuf, zbuf, stage, acc,
    psend, precv, y2send, y2recv, ysend, yrecv, zsend, zrecv,
):
    row, far, core = place()
    up, dn = slot_of(row + 1, far, core), slot_of(row - 1, far, core)
    anti, sib = slot_of(row, 1 - far, core), slot_of(row, far, 1 - core)
    nbr = (narrow_id(up), narrow_id(dn))
    anti_id, sib_id = narrow_id(anti), narrow_id(sib)
    half = {0: (0, 1), 1: (2, 3)}
    arrive = hello((*nbr, anti_id, sib_id))
    loads = [
        pltpu.make_async_copy(gown_in, gown, lsem.at[0]),
        pltpu.make_async_copy(amat_in, amat, lsem.at[1]),
    ]
    for c in loads:
        c.start()
    columns(rev, col)

    shape = (512, 256)
    at = lax.broadcasted_iota(jnp.int32, shape, 0)
    named = ((lax.rem(lax.div(at, 32), 4) * 2 + lax.rem(lax.div(at, 128), 2)) * 2 + lax.div(at, 256)) * 32
    named = (named + lax.rem(at, 32)).astype(jnp.float32)
    hot[...] = jnp.where(named == slot_row(src, cnt), 1.0, 0.0).astype(jnp.bfloat16)
    tile = 512

    def tiles(i, carry):
        sl = pl.ds(pl.multiple_of(i * tile, tile), tile)
        theirs = pick_rows(col[sl, :], got[...])
        grad = (gown[sl, :] + theirs + swap_halves(theirs)).astype(jnp.bfloat16)
        for k in range(tile // 64):
            a = amat[pl.ds(pl.multiple_of(i * tile + k * 64, 64), 64), :]
            pair = paired(dot_cols(a, grad[k * 64 : k * 64 + 64]))
            for s in range(8):
                to = pl.multiple_of((s * 32 + i * (tile // 64) + k) * 32, 32)
                pairs[pl.ds(to, 32), :] = pair[s * 32 : s * 32 + 32]
        return carry

    for c in loads:
        c.wait()
    lax.fori_loop(0, gown.shape[0] // tile, tiles, 0)
    copies = []

    def go(c):
        c.start()
        copies.append(c)
        return c

    sc, y2, yc, zc = {}, {}, {}, {}
    far_of = (1 - far, far)
    bf = jnp.bfloat16

    def build(q):
        def one(g, carry):
            t = [pairs[pl.ds(g * 2 + e, 256, stride=32), :].astype(bf) for e in (0, 1)]
            both = dot(hot[...], jnp.concatenate(t, axis=1)).astype(bf)
            for e in (0, 1):
                parts[g * 2 + e] = both[:, e * 128 : e * 128 + 128]
            return carry

        lax.fori_loop(4 * q, 4 * q + 4, one, 0)
        sl = pl.ds(8 * q, 8)
        mate = pl.ds(pl.multiple_of((1 - core) * 256, 256), 256)
        sc[q] = go(send(parts.at[sl, mate], near_buf.at[sl], psend.at[q], precv.at[q], sib_id))

    def chip_sum(z, o, q):
        sl = pl.ds(8 * q, 8)
        to = far_of[z] * 128 + lax.rem(row + o, 4) * 32
        a = parts[sl, pl.ds(pl.multiple_of(core * 256 + to, 32), 32), :]
        b = near_buf[sl, pl.ds(pl.multiple_of(to, 32), 32), :]
        return a.astype(jnp.float32) + b.astype(jnp.float32)

    def first(z, q):
        sl = pl.ds(8 * q, 8)
        d = 0 if q in half[0] else 1
        stage[z, 2, sl] = chip_sum(z, 2, q).astype(bf)
        y2[z, q] = go(send(stage.at[z, 2, sl], y2buf.at[z, sl], y2send.at[z, q], y2recv.at[z, q], nbr[d]))
        e = 1 - d
        o = 1 if e == 0 else 3
        stage[z, o, sl] = chip_sum(z, o, q).astype(bf)
        yc[z, e, q] = go(send(stage.at[z, o, sl], ybuf.at[z, e, sl], ysend.at[z, e, q], yrecv.at[z, e, q], nbr[e]))

    def second(z, q):
        sl = pl.ds(8 * q, 8)
        d = 0 if q in half[0] else 1
        o = 1 if d == 0 else 3
        y2[z, q].wait_recv()
        stage[z, o, sl] = (chip_sum(z, o, q) + y2buf[z, sl].astype(jnp.float32)).astype(bf)
        yc[z, d, q] = go(send(stage.at[z, o, sl], ybuf.at[z, d, sl], ysend.at[z, d, q], yrecv.at[z, d, q], nbr[d]))

    def final(z, q):
        sl = pl.ds(8 * q, 8)
        yc[z, 0, q].wait_recv()
        yc[z, 1, q].wait_recv()
        return (
            chip_sum(z, 0, q)
            + ybuf[z, 0, sl].astype(jnp.float32)
            + ybuf[z, 1, sl].astype(jnp.float32)
        )

    order = (0, 2, 1, 3)
    arrive()
    build(order[0])
    for i in range(CH):
        if i + 1 < CH:
            build(order[i + 1])
        sc[order[i]].wait_recv()
        first(0, order[i])
    for q in order:
        second(0, q)
        first(1, q)
    for q in order:
        sl = pl.ds(8 * q, 8)
        stage[0, 0, sl] = final(0, q).astype(bf)
        zc[q] = go(send(stage.at[0, 0, sl], zbuf.at[sl], zsend.at[q], zrecv.at[q], anti_id))
        second(1, q)
    for q in order:
        acc[pl.ds(8 * q, 8)] = final(1, q)
    for q in order:
        sl = pl.ds(8 * q, 8)
        zc[q].wait_recv()
        total = acc[sl] + zbuf[sl].astype(jnp.float32)
        for r in range(8):
            out[pl.ds(8 * q + r, 32, stride=32), :] = total[r]
    for c in copies:
        c.wait_send()


def back(src, cnt, rev, got, gown, amat):
    dma = pltpu.SemaphoreType.DMA
    vm = pltpu.VMEM
    bf, f32 = jnp.bfloat16, jnp.float32
    inside = pl.BlockSpec(memory_space=vm)
    return pl.pallas_call(
        back_kernel,
        name="back",
        in_specs=[inside] * 4 + [pl.BlockSpec(memory_space=pl.ANY)] * 2,
        out_specs=inside,
        out_shape=jax.ShapeDtypeStruct((1024, 128), f32),
        scratch_shapes=[
            vm(gown.shape, f32),
            vm(amat.shape, bf),
            dma((2,)),
            vm((2048, 1), jnp.int32),
            vm((8192, 128), f32),
            vm((512, 256), bf),
            vm((32, 512, 128), bf),
            vm((32, 256, 128), bf),
            vm((2, 32, 32, 128), bf),
            vm((2, 2, 32, 32, 128), bf),
            vm((32, 32, 128), bf),
            vm((2, 4, 32, 32, 128), bf),
            vm((32, 32, 128), f32),
            dma((CH,)),
            dma((CH,)),
            dma((2, CH)),
            dma((2, CH)),
            dma((2, 2, CH)),
            dma((2, 2, CH)),
            dma((CH,)),
            dma((CH,)),
        ],
        compiler_params=pltpu.CompilerParams(collective_id=1, has_side_effects=True),
    )(src, cnt, rev, got, gown, amat)


def last_kernel(gmsg, total, pre, down, res, out, res_out):
    res_out[...] = res[...]
    grad = (total[...] * silu_both(pre[...])[1]).astype(jnp.bfloat16)
    w = jnp.concatenate([down[...]] * 2, axis=0)
    out[...] = (gmsg[...].astype(jnp.float32) + dot(spread(grad), w)).astype(jnp.bfloat16)


def last(gmsg, total, pre, down, res):
    n, d = gmsg.shape
    t = n // LAST_TILES
    wide = pl.BlockSpec((t, d), lambda i: (i, 0))
    slim = pl.BlockSpec((t // 2, 128), lambda i: (i, 0))
    return pl.pallas_call(
        last_kernel,
        name="last",
        grid=(LAST_TILES,),
        in_specs=[wide, slim, slim, pl.BlockSpec(down.shape, lambda i: (0, 0)), wide],
        out_specs=[wide, wide],
        out_shape=[jax.ShapeDtypeStruct((n, d), jnp.bfloat16)] * 2,
    )(gmsg, total, pre, down, res)


def on_device(x, cot, down, up, inner, outer, ang, reverse, sources, counts):
    down, src = down.T, sources.T
    rev = reverse.reshape(-1, 128)
    theirs, pre, amat, ups, slopes = front(src, counts, x, down, up, ang)
    res, gmsg, got, gown = layer(x, cot, ups, slopes, theirs, rev, up, inner[0], outer[0])
    total = back(src, counts.reshape(1, -1), rev, got, gown, amat)
    grad_x, out = last(gmsg, total, pre, down, res)
    return out, grad_x


def solution(mesh):
    rows = P(("cluster", "narrow"))
    specs = (rows, rows, P(), P(), P(), P(), rows, rows, rows, rows)
    return jax.shard_map(
        on_device, mesh=mesh, in_specs=specs, out_specs=(rows, rows), check_vma=False
    )
```
